512 devices in a mesh: gy: 16 (over z, core), gx: 32 (over y, x).
Axes of the slice: x: 4, y: 8, z: 8, core: 2. Of those that a mesh axis runs over, the one named last changes fastest.
Arguments:
- mask: float32 [640, 4096], P('gy', 'gx'), may hold values from 0 to 1
- target: int32 [640, 4096], P('gy', 'gx'), may hold values 0 or 1
- kernels: bfloat16 [24, 35, 35], replicated, may hold values from -0.15625 to 0.15625
- offsets: int32 [8, 2], replicated, may hold values from -8 to 8, as said below
- load_weights: float32 [8], replicated, may hold values from 0.2 to 1
Outputs:
- update: float32 [640, 4096], P('gy', 'gx')
- loss: float32 [], replicated
The draws below stay inside these ranges and needn't reach their ends.
Inputs may be any that keep to these rules, and one draw needn't show every extreme that they name: `offsets`: some offset has row component 8 and some has column component -8.
All inputs are finite; a program needn't handle non-finite values. No bound on the sum of `target` on one device may be relied on, other than what follows from the above.
Results may differ from the reference program's by a relative error of at most 0.002.
Values may be sent and summed in bfloat16 or wider, within the bound.
A program may use at most 64 MiB of HBM per device.

```python
import math
import jax
import jax.numpy as jnp
from jax import lax

KERNELS = 12
TAPS = 35
REACH = 8
LOAD_TAPS = 8
ROWS = 640
COLS = 4096


def draw_offsets(key, part):
    drawn = jax.random.randint(jax.random.fold_in(key, 11), (LOAD_TAPS, 2), -REACH, REACH + 1)
    drawn = drawn.at[0, 0].set(REACH)
    drawn = drawn.at[1, 1].set(-REACH)
    return drawn.astype(jnp.int32)


def with_ends(entries, rng, least, top_value):
    dims = entries.shape
    place = [jax.random.randint(jax.random.fold_in(rng, axis), (), 0, dims[axis]) for axis in range(len(dims))]
    entries = entries.at[tuple(place)].set(least)
    longest = dims.index(max(dims))
    place[longest] = (place[longest] + 1) % dims[longest]
    return entries.at[tuple(place)].set(top_value)


def level_of(key, dims, shards, low, top_value):
    level = 1.0
    for dim, shards_of in shards:
        steps = jax.random.uniform(jax.random.fold_in(jax.random.fold_in(key, 6), dim), (shards_of,), jnp.float32, low / len(shards), top_value / len(shards))
        level = level * jnp.repeat(jnp.exp(steps), dims[dim] // shards_of).reshape((-1,) + (1,) * (len(dims) - 1 - dim))
    return level


def centred(stream_key, dims, deviation, most, kind=jnp.bfloat16):
    return jnp.clip(deviation * jax.random.normal(stream_key, dims, jnp.float32), -most, most).astype(kind)


def setup_inputs(seed: int = 0) -> dict:
    key_list = jax.random.split(jax.random.key(seed), 6)
    mask = jnp.clip(1.0 * jax.random.uniform(key_list[0], (ROWS, COLS), jnp.float32) ** level_of(key_list[0], (ROWS, COLS), ((0, 16), (1, 32)), -0.2, 0.2), 0.0, 1.0)
    target = with_ends((jax.random.randint(key_list[1], (ROWS, COLS), 0, 2) < 1).astype(jnp.int32), jax.random.fold_in(key_list[1], 1), 0, 1)
    kernels = centred(key_list[2], (2 * KERNELS, TAPS, TAPS), (TAPS * TAPS) ** -0.5, 0.15625)
    offsets = draw_offsets(jax.random.fold_in(key_list[5], 71), 0)
    load_weights = jnp.clip(jnp.exp(jax.random.uniform(key_list[4], (LOAD_TAPS,), jnp.float32, math.log(0.2), math.log(1.0))), 0.2, 1.0)
    return {"mask": mask, "target": target, "kernels": kernels, "offsets": offsets, "load_weights": load_weights}


SMOOTH_TAPS = (0.0625, 0.25, 0.375, 0.25, 0.0625)
SHARPNESS = 4.0
THRESHOLD = 0.65
LOADING_GAIN = 0.5

def smooth_same(values):
    padded = jnp.pad(values, 2)
    height, width = values.shape
    partial_rows = sum((SMOOTH_TAPS[a] * padded[a:a + height, :] for a in range(5)))
    return sum((SMOOTH_TAPS[b] * partial_rows[:, b:b + width] for b in range(5)))

def correlate(field, weights, radius):
    return lax.conv_general_dilated(field[None], weights, (1, 1), [(radius, radius), (radius, radius)], dimension_numbers=('NCHW', 'OIHW', 'NCHW'), precision=lax.Precision.HIGHEST)[0]

def reference(mask, target, kernels, offsets, load_weights):
    height, width = mask.shape
    radius = kernels.shape[-1] // 2
    plane = mask.astype(jnp.bfloat16).astype(jnp.float32)
    forward_weights = kernels.astype(jnp.float32)[:, None]
    field = correlate(plane[None], forward_weights, radius)
    intensity = lax.optimization_barrier(jnp.sum(field * field, axis=0)) / KERNELS
    dense = smooth_same(intensity)
    develop = jax.nn.sigmoid(SHARPNESS * (dense - THRESHOLD))
    padded = jnp.pad(develop, REACH)
    loading = jnp.zeros((height, width), jnp.float32)
    for index in range(LOAD_TAPS):
        start_row = (REACH + offsets[index, 0]).astype(jnp.int32)
        start_col = (REACH + offsets[index, 1]).astype(jnp.int32)
        loading = loading + load_weights[index] * lax.dynamic_slice(padded, (start_row, start_col), (height, width))
    printed = develop - LOADING_GAIN / LOAD_TAPS * loading
    row_pos = jnp.arange(height, dtype=jnp.float32)
    col_pos = jnp.arange(width, dtype=jnp.float32)
    weight = (1.0 + 2.0 * row_pos / height)[:, None] * (1.0 + 2.0 * col_pos / width)[None, :]
    diff = printed - target.astype(jnp.float32)
    loss = jnp.sum(weight * diff * diff)
    resid = 2.0 * weight * diff
    resid_pad = jnp.pad(resid, REACH)
    back = jnp.zeros((height, width), jnp.float32)
    for index in range(LOAD_TAPS):
        start_row = (REACH - offsets[index, 0]).astype(jnp.int32)
        start_col = (REACH - offsets[index, 1]).astype(jnp.int32)
        back = back + load_weights[index] * lax.dynamic_slice(resid_pad, (start_row, start_col), (height, width))
    slope = resid - LOADING_GAIN / LOAD_TAPS * back
    dense_grad = slope * SHARPNESS * develop * (1.0 - develop)
    inten_grad = smooth_same(dense_grad)
    products = lax.optimization_barrier((2.0 * field * inten_grad / KERNELS).astype(jnp.bfloat16)).astype(jnp.float32)
    adjoint_weights = jnp.transpose(forward_weights[:, :, ::-1, ::-1], (1, 0, 2, 3))
    gradient = correlate(products, adjoint_weights, radius)[0]
    scale = jnp.sqrt(jnp.sum(gradient * gradient) / (height * width) + 1e-06)
    update = mask - gradient / scale
    return (update, loss)
```

```python
import functools

import jax
import jax.numpy as jnp
from jax import lax
from jax.experimental import pallas as pl
from jax.experimental.pallas import tpu as pltpu
from jax.sharding import PartitionSpec as P

MESH = pl.DeviceIdType.MESH
F32 = jnp.float32
BF16 = jnp.bfloat16

KERNELS = 12
CHANNELS = 24
TAPS = 35
REACH = 8
LOAD_TAPS = 8
SMOOTH_TAPS = (0.0625, 0.25, 0.375, 0.25, 0.0625)
SHARPNESS = 4.0
THRESHOLD = 0.65
LOADING_GAIN = 0.5

ROWS, COLS = 40, 128
LANES = 256
FIELD_MARGIN = 37
PLANE_MARGIN = 54
PITCH = 40
BAND = 8
DEPTH = 1792
BANDS = 15
FIRST_BAND, LAST_BAND = 2, 11


def lane_index(rows, lanes=LANES):
    return lax.broadcasted_iota(jnp.int32, (rows, lanes), 1)


def row_index(rows, lanes=LANES):
    return lax.broadcasted_iota(jnp.int32, (rows, lanes), 0)


def smooth(ref, start, rows):
    down = sum(SMOOTH_TAPS[a] * ref[pl.ds(start + a - 2, rows), :] for a in range(5))
    total = SMOOTH_TAPS[2] * down
    for b in (0, 1, 3, 4):
        total = total + SMOOTH_TAPS[b] * pltpu.roll(down, (2 - b) % LANES, 1)
    return total


def rows_from(halves, start, rows):
    return jnp.concatenate([halves[i, pl.ds(start, rows), :] for i in range(2)], axis=1)


def build_taps(kernels_ref, flipped, base, taps32, taps, mixer32, mixer):
    flip = (
        lax.broadcasted_iota(jnp.int32, (TAPS, 128), 0) + lax.broadcasted_iota(jnp.int32, (TAPS, 128), 1) == TAPS - 1
    ).astype(BF16)
    for c in range(CHANNELS):
        flipped[c * PITCH : c * PITCH + TAPS, :] = jnp.dot(kernels_ref[c], flip, preferred_element_type=F32)
    lane = lane_index(CHANNELS, 128)
    tiles = [jnp.zeros((CHANNELS, 128), F32) for _ in range(DEPTH // 128)]
    for a in range(TAPS):
        tile, shift = divmod(a * PITCH, 128)
        row = flipped[pl.ds(a, CHANNELS, stride=PITCH), :]
        moved = pltpu.roll(row, shift, 1) if shift else row
        tiles[tile] = tiles[tile] + jnp.where(lane >= shift, moved, 0.0)
        if shift + TAPS > 128:
            tiles[tile + 1] = tiles[tile + 1] + jnp.where(lane < shift, moved, 0.0)
    for i, tile in enumerate(tiles):
        base[:, i * 128 : (i + 1) * 128] = tile
    for y in range(BAND):
        moved = base[...]
        if y:
            moved = pltpu.roll(moved, y * PITCH, 1)
        for i in range(DEPTH // 128):
            taps32[i, pl.ds(y, CHANNELS, stride=BAND), :] = moved[:, i * 128 : (i + 1) * 128]
    joined = jnp.concatenate([taps32[i] for i in range(DEPTH // 128)], axis=1)
    taps[...] = joined.astype(BF16)
    rows = CHANNELS * BAND
    for n in range(6):
        first = (PLANE_MARGIN - 8 * (n + 2)) * PITCH
        low, high = max(first, 0), min(first + 8 * PITCH, DEPTH)
        window = joined[:, low:high]
        if first < 0:
            window = jnp.concatenate([jnp.zeros((rows, -first), F32), window], axis=1)
        if high < first + 8 * PITCH:
            window = jnp.concatenate([window, jnp.zeros((rows, first + 8 * PITCH - high), F32)], axis=1)
        mixer32[n * rows : (n + 1) * rows, 0 : 8 * PITCH] = window
    mixer[...] = mixer32[...].T[0 : 8 * PITCH, :].astype(BF16)


def kernel(
    sizes,
    offsets_ref,
    weights_ref,
    mask_ref,
    target_ref,
    kernels_ref,
    update_ref,
    loss_ref,
    whole,
    edges,
    rims,
    got_whole,
    got_edges,
    got_rims,
    sums_y,
    sums_x,
    flipped,
    base,
    taps32,
    taps,
    mixer32,
    mixer,
    plane,
    wanted,
    patches,
    field,
    buf_a,
    buf_b,
    buf_c,
    halves_b,
    halves_c,
    products,
    mixed,
    send_sem,
    recv_sem,
    sum_send,
    sum_recv,
):
    ny, nx = sizes
    gy, gx = lax.axis_index("gy"), lax.axis_index("gx")

    def at(dy, dx):
        return (lax.rem(gy + (dy % ny), ny), lax.rem(gx + (dx % nx), nx))

    peers = {(dy % ny, dx % nx) for dy in range(-2, 3) for dx in range(-1, 2)}
    peers |= {(d, 0) for d in range(ny)} | {(0, d) for d in range(nx)}
    peers = sorted(peers - {(0, 0)})
    barrier = pltpu.get_barrier_semaphore()
    for dy, dx in peers:
        pl.semaphore_signal(barrier, inc=1, device_id=at(dy, dx), device_id_type=MESH)

    own_plane = mask_ref[...].astype(BF16).astype(F32)
    own_target = target_ref[...].astype(F32)
    lane = lane_index(ROWS, 128)
    whole[0] = own_plane.astype(BF16)
    whole[1] = own_target.astype(BF16)
    left = jnp.where(lane < 64, own_plane, pltpu.roll(own_target, 64, 1))
    right = jnp.where(lane < 64, pltpu.roll(own_plane, 54, 1), pltpu.roll(own_target, 91, 1))
    edges[0] = left.astype(BF16)
    edges[1] = right.astype(BF16)
    for i, value in enumerate((right, own_plane, left)):
        rims[i, 0] = value[24:40, :].astype(BF16)
        rims[i, 1] = value[0:16, :].astype(BF16)

    build_taps(kernels_ref, flipped, base, taps32, taps, mixer32, mixer)

    pl.semaphore_wait(barrier, len(peers))

    copies = []

    def send(source, target, dy, dx):
        slot = len(copies)
        copies.append(
            pltpu.make_async_remote_copy(
                src_ref=source,
                dst_ref=target,
                send_sem=send_sem.at[slot],
                recv_sem=recv_sem.at[slot],
                device_id=at(dy, dx),
                device_id_type=MESH,
            )
        )
        copies[-1].start()

    for dx in (1, -1):
        side = 1 if dx == 1 else 0
        for dy in (-1, 0, 1):
            send(edges.at[side], got_edges.at[0 if dx == 1 else 1, 1 - dy], dy, dx)
    for dx in (1, -1, 0):
        for dy in (2, -2):
            end = 0 if dy == 2 else 1
            send(rims.at[1 - dx, end], got_rims.at[1 - dx, end], dy, dx)
    for dy in (1, -1):
        send(whole, got_whole.at[0 if dy == 1 else 1], dy, 0)
    for copy in copies:
        copy.wait()

    first_row = gy * ROWS
    first_col = gx * COLS
    total_rows, total_cols = ny * ROWS, nx * COLS

    def framed(row, rows, middle, west, east):
        n = lane_index(rows, 128)
        moved = pltpu.roll(middle, PLANE_MARGIN, 1)
        low = jnp.where(n < PLANE_MARGIN, west, moved)
        high = jnp.where(n < PLANE_MARGIN, moved, jnp.where(n < 2 * PLANE_MARGIN, pltpu.roll(east, 54, 1), 0.0))
        value = jnp.concatenate([low, high], axis=1)
        y = first_row - PLANE_MARGIN - 2 + row + row_index(rows)
        x = first_col - PLANE_MARGIN + lane_index(rows)
        inside = (y >= 0) & (y < total_rows) & (x >= 0) & (x < total_cols)
        plane[row : row + rows, :] = pltpu.roll(jnp.where(inside, value, 0.0), LANES - TAPS + 1, 1)

    def wide(value):
        return value.astype(F32)

    framed(0, 16, wide(got_rims[1, 0]), wide(got_rims[0, 0]), wide(got_rims[2, 0]))
    framed(16, 40, wide(got_whole[0, 0]), wide(got_edges[0, 0]), wide(got_edges[1, 0]))
    framed(56, 40, own_plane, wide(got_edges[0, 1]), wide(got_edges[1, 1]))
    framed(96, 40, wide(got_whole[1, 0]), wide(got_edges[0, 2]), wide(got_edges[1, 2]))
    framed(136, 16, wide(got_rims[1, 1]), wide(got_rims[0, 1]), wide(got_rims[2, 1]))
    plane[152:160, :] = jnp.zeros((8, LANES), F32)

    def framed_target(row, middle, west, east):
        n = lane_index(ROWS, 128)
        moved = pltpu.roll(middle, FIELD_MARGIN, 1)
        wanted[row : row + ROWS, 0:128] = jnp.where(n < FIELD_MARGIN, pltpu.roll(west, 74, 1), moved)
        wanted[row : row + ROWS, 128:256] = jnp.where(n < FIELD_MARGIN, moved, pltpu.roll(east, 101, 1))

    framed_target(0, wide(got_whole[0, 1]), wide(got_edges[0, 0]), wide(got_edges[1, 0]))
    framed_target(40, own_target, wide(got_edges[0, 1]), wide(got_edges[1, 1]))
    framed_target(80, wide(got_whole[1, 1]), wide(got_edges[0, 2]), wide(got_edges[1, 2]))

    def spread(step, carry):
        pieces = []
        for i in range(2):
            row = plane[pl.ds(step * 2 + i + 2, 1), :]
            row = jnp.broadcast_to(row, (PITCH, LANES))
            pieces.append(pltpu.roll(row, 0, 1, stride=1, stride_axis=0))
        value = jnp.concatenate(pieces, axis=0).astype(BF16)
        patches[pl.ds(pl.multiple_of(step * 2 * PITCH, 2 * PITCH), 2 * PITCH), :] = value
        return carry

    lax.fori_loop(0, 79, spread, 0)

    def inside_field(start, rows):
        y = first_row - FIELD_MARGIN + start + row_index(rows)
        x = first_col - FIELD_MARGIN + lane_index(rows)
        return (y >= 0) & (y < total_rows) & (x >= 0) & (x < total_cols)

    for ref in (buf_a, buf_b, buf_c):
        ref[0:8, :] = jnp.zeros((8, LANES), F32)
        ref[8 + BANDS * BAND :, :] = jnp.zeros((8, LANES), F32)

    def band(i, carry):
        rows = pl.ds(pl.multiple_of(i * BAND * PITCH, BAND * PITCH), DEPTH)
        value = jnp.dot(taps[...], patches[rows, :], preferred_element_type=F32)
        value = value.reshape(CHANNELS, BAND, LANES)
        start = pl.multiple_of(i * BAND, BAND)
        field[:, pl.ds(start, BAND), :] = value
        intensity = jnp.sum(value * value, axis=0) / KERNELS
        buf_a[pl.ds(start + 8, BAND), :] = jnp.where(inside_field(start, BAND), intensity, 0.0)
        return carry

    lax.fori_loop(0, BANDS, band, 0)

    dense = smooth(buf_a, 8, 120)
    develop = jnp.where(inside_field(0, 120), jax.nn.sigmoid(SHARPNESS * (dense - THRESHOLD)), 0.0)
    buf_b[8:128, :] = develop
    for i in range(2):
        halves_b[i, 8:128, :] = develop[:, i * 128 : (i + 1) * 128]
        halves_b[i, 0:8, :] = jnp.zeros((8, 128), F32)
        halves_b[i, 128:136, :] = jnp.zeros((8, 128), F32)

    loading = jnp.zeros((104, LANES), F32)
    for j in range(LOAD_TAPS):
        part = rows_from(halves_b, 16 + offsets_ref[j, 0], 104)
        loading = loading + weights_ref[j] * pltpu.roll(part, lax.rem(LANES - offsets_ref[j, 1], LANES), 1)
    printed = buf_b[16:120, :] - LOADING_GAIN / LOAD_TAPS * loading
    y = first_row - FIELD_MARGIN + 8 + row_index(104)
    x = first_col - FIELD_MARGIN + lane_index(104)
    weight = (1.0 + 2.0 * y.astype(F32) / total_rows) * (1.0 + 2.0 * x.astype(F32) / total_cols)
    diff = printed - wanted[11:115, :]
    own = (y >= first_row) & (y < first_row + ROWS) & (x >= first_col) & (x < first_col + COLS)
    loss = jnp.sum(jnp.where(own, weight * diff * diff, 0.0), axis=0, keepdims=True)
    resid = jnp.where(inside_field(8, 104), 2.0 * weight * diff, 0.0)
    buf_c[16:120, :] = resid
    for i in range(2):
        halves_c[i, 16:120, :] = resid[:, i * 128 : (i + 1) * 128]

    back = jnp.zeros((88, LANES), F32)
    for j in range(LOAD_TAPS):
        part = rows_from(halves_c, 24 - offsets_ref[j, 0], 88)
        back = back + weights_ref[j] * pltpu.roll(part, lax.rem(LANES + offsets_ref[j, 1], LANES), 1)
    slope = buf_c[24:112, :] - LOADING_GAIN / LOAD_TAPS * back
    nearby = buf_b[24:112, :]
    buf_a[24:112, :] = slope * SHARPNESS * nearby * (1.0 - nearby)
    pull = smooth(buf_a, 24, 80)
    buf_b[24:104, :] = jnp.where(inside_field(16, 80), pull, 0.0)

    def weigh(i, carry):
        start = pl.multiple_of((i + FIRST_BAND) * BAND, BAND)
        value = 2.0 * field[:, pl.ds(start, BAND), :] * buf_b[pl.ds(start + 8, BAND), :][None] / KERNELS
        rows = pl.ds(pl.multiple_of(i * CHANNELS * BAND, CHANNELS * BAND), CHANNELS * BAND)
        products[rows, :] = value.reshape(CHANNELS * BAND, LANES).astype(BF16)
        return carry

    lax.fori_loop(0, LAST_BAND - FIRST_BAND + 1, weigh, 0)

    def mix(g, carry):
        rows = pl.ds(pl.multiple_of(g * CHANNELS * BAND, CHANNELS * BAND), 6 * CHANNELS * BAND)
        value = jnp.dot(mixer[...], products[rows, :], preferred_element_type=F32)
        for i in range(2):
            mixed[i, pl.ds(pl.multiple_of(g * 8 * PITCH, 8 * PITCH), 8 * PITCH), :] = value[:, i * 128 : (i + 1) * 128]
        return carry

    lax.fori_loop(0, ROWS // 8, mix, 0)

    gradient = jnp.zeros((ROWS, 128), F32)
    for t in range(TAPS):
        part = jnp.concatenate([mixed[i, pl.ds(t, ROWS, stride=PITCH), :] for i in range(2)], axis=1)
        gradient = gradient + pltpu.roll(part, 236 - t, 1)[:, 0:128]

    def gather(sums, axis_size, me, number):
        out = []
        for d in range(1, axis_size):
            peer = lax.rem(me + d, axis_size)
            out.append(
                pltpu.make_async_remote_copy(
                    src_ref=sums.at[me],
                    dst_ref=sums.at[me],
                    send_sem=sum_send.at[number, d],
                    recv_sem=sum_recv.at[number, d],
                    device_id=(peer, gx) if number == 0 else (gy, peer),
                    device_id_type=MESH,
                )
            )
            out[-1].start()
        for copy in out:
            copy.wait()

    square = jnp.sum(gradient * gradient, axis=0, keepdims=True)
    sums_y[gy, 0:1, :] = loss[:, 0:128] + loss[:, 128:256]
    sums_y[gy, 1:2, :] = square
    gather(sums_y, ny, gy, 0)
    sums_x[gx] = jnp.sum(sums_y[...], axis=0)
    gather(sums_x, nx, gx, 1)
    totals = jnp.sum(jnp.sum(sums_x[...], axis=0), axis=1, keepdims=True)
    loss_ref[...] = totals[0:1, :]
    scale = jnp.sqrt(totals[1:2, :] / (total_rows * total_cols) + 1e-06)
    update_ref[...] = mask_ref[...] - gradient / scale


def solution(mesh):
    ny, nx = mesh.shape["gy"], mesh.shape["gx"]
    vmem = pl.BlockSpec(memory_space=pltpu.VMEM)
    smem = pl.BlockSpec(memory_space=pltpu.SMEM)
    rows = CHANNELS * BAND

    def step(mask, target, kernels, offsets, load_weights):
        update, loss = pl.pallas_call(
            functools.partial(kernel, (ny, nx)),
            out_shape=(
                jax.ShapeDtypeStruct((ROWS, COLS), F32),
                jax.ShapeDtypeStruct((1, 1), F32),
            ),
            in_specs=[smem, smem, vmem, vmem, vmem],
            out_specs=(vmem, vmem),
            scratch_shapes=[
                pltpu.VMEM((2, ROWS, COLS), BF16),
                pltpu.VMEM((2, ROWS, COLS), BF16),
                pltpu.VMEM((3, 2, 16, COLS), BF16),
                pltpu.VMEM((2, 2, ROWS, COLS), BF16),
                pltpu.VMEM((2, 3, ROWS, COLS), BF16),
                pltpu.VMEM((3, 2, 16, COLS), BF16),
                pltpu.VMEM((ny, 2, 128), F32),
                pltpu.VMEM((nx, 2, 128), F32),
                pltpu.VMEM((CHANNELS * PITCH, 128), F32),
                pltpu.VMEM((CHANNELS, DEPTH), F32),
                pltpu.VMEM((DEPTH // 128, rows, 128), F32),
                pltpu.VMEM((rows, DEPTH), BF16),
                pltpu.VMEM((6 * rows, 384), F32),
                pltpu.VMEM((8 * PITCH, 6 * rows), BF16),
                pltpu.VMEM((160, LANES), F32),
                pltpu.VMEM((120, LANES), F32),
                pltpu.VMEM((6320, LANES), BF16),
                pltpu.VMEM((CHANNELS, BANDS * BAND, LANES), F32),
                pltpu.VMEM((136, LANES), F32),
                pltpu.VMEM((136, LANES), F32),
                pltpu.VMEM((136, LANES), F32),
                pltpu.VMEM((2, 136, 128), F32),
                pltpu.VMEM((2, 136, 128), F32),
                pltpu.VMEM((10 * rows, LANES), BF16),
                pltpu.VMEM((2, ROWS * PITCH, 128), F32),
                pltpu.SemaphoreType.DMA((14,)),
                pltpu.SemaphoreType.DMA((14,)),
                pltpu.SemaphoreType.DMA((2, 32)),
                pltpu.SemaphoreType.DMA((2, 32)),
            ],
            compiler_params=pltpu.CompilerParams(collective_id=0, has_side_effects=True),
        )(offsets, load_weights, mask, target, kernels)
        return update, loss[0, 0]

    placed = (P("gy", "gx"), P("gy", "gx"), P(), P(), P())
    return jax.shard_map(step, mesh=mesh, in_specs=placed, out_specs=(P("gy", "gx"), P()), check_vma=False)
```

```python
import functools

import jax
import jax.numpy as jnp
from jax import lax
from jax.experimental import pallas as pl
from jax.experimental.pallas import tpu as pltpu
from jax.sharding import PartitionSpec as P

MESH = pl.DeviceIdType.MESH
F32 = jnp.float32
BF16 = jnp.bfloat16

KERNELS = 12
CHANNELS = 24
TAPS = 35
REACH = 8
LOAD_TAPS = 8
SMOOTH_TAPS = (0.0625, 0.25, 0.375, 0.25, 0.0625)
SHARPNESS = 4.0
THRESHOLD = 0.65
LOADING_GAIN = 0.5

ROWS, COLS = 40, 128
LANES = 256
FIELD_MARGIN = 37
PLANE_MARGIN = 54
PITCH = 36
BAND = 8
DEPTH = 1536
BANDS = 15
FIRST_BAND, LAST_BAND = 2, 11


def lane_index(rows, lanes=LANES):
    return lax.broadcasted_iota(jnp.int32, (rows, lanes), 1)


def row_index(rows, lanes=LANES):
    return lax.broadcasted_iota(jnp.int32, (rows, lanes), 0)


def smooth(ref, start, rows):
    down = sum(SMOOTH_TAPS[a] * ref[pl.ds(start + a - 2, rows), :] for a in range(5))
    total = SMOOTH_TAPS[2] * down
    for b in (0, 1, 3, 4):
        total = total + SMOOTH_TAPS[b] * pltpu.roll(down, (2 - b) % LANES, 1)
    return total


def rows_from(halves, start, rows):
    return jnp.concatenate([halves[i, pl.ds(start, rows), :] for i in range(2)], axis=1)


def build_taps(kernels_ref, taps32, taps):
    flip = (
        lax.broadcasted_iota(jnp.int32, (TAPS, 128), 0) + lax.broadcasted_iota(jnp.int32, (TAPS, 128), 1) == TAPS - 1
    ).astype(BF16)
    lane = lane_index(CHANNELS, 128)
    tiles = [jnp.zeros((CHANNELS, 128), F32) for _ in range(DEPTH // 128)]
    for a in range(TAPS):
        tile, shift = divmod(a * PITCH, 128)
        row = jnp.dot(kernels_ref[a], flip, preferred_element_type=F32)
        moved = pltpu.roll(row, shift, 1) if shift else row
        tiles[tile] = tiles[tile] + jnp.where(lane >= shift, moved, 0.0)
        if shift + TAPS > 128:
            tiles[tile + 1] = tiles[tile + 1] + jnp.where(lane < shift, moved, 0.0)
    base = jnp.concatenate(tiles, axis=1)
    for y in range(BAND):
        moved = pltpu.roll(base, y * PITCH, 1) if y else base
        for i in range(DEPTH // 128):
            taps32[i, pl.ds(y, CHANNELS, stride=BAND), :] = moved[:, i * 128 : (i + 1) * 128]
    for i in range(DEPTH // 128):
        taps[:, i * 128 : (i + 1) * 128] = taps32[i].astype(BF16)


def build_mixer(taps32, mixer32, mixer):
    joined = jnp.concatenate([taps32[i] for i in range(DEPTH // 128)], axis=1)
    rows = CHANNELS * BAND
    for n in range(6):
        first = (PLANE_MARGIN - 8 * (n + 2)) * PITCH
        low, high = max(first, 0), min(first + 8 * PITCH, DEPTH)
        window = joined[:, low:high]
        if first < 0:
            window = jnp.concatenate([jnp.zeros((rows, -first), F32), window], axis=1)
        if high < first + 8 * PITCH:
            window = jnp.concatenate([window, jnp.zeros((rows, first + 8 * PITCH - high), F32)], axis=1)
        mixer32[n * rows : (n + 1) * rows, 0 : 8 * PITCH] = window
    mixer[...] = mixer32[...].T[0 : 8 * PITCH, :].astype(BF16)


def kernel(
    sizes,
    offsets_hbm,
    weights_hbm,
    mask_hbm,
    target_hbm,
    kernels_hbm,
    update_ref,
    loss_ref,
    offsets_ref,
    weights_ref,
    mask_ref,
    target_ref,
    kernels_ref,
    input_sem,
    whole,
    edges,
    rims,
    got_whole,
    got_edges,
    got_rims,
    sums_y,
    sums_x,
    taps32,
    taps,
    mixer32,
    mixer,
    plane,
    wanted,
    patches,
    field,
    buf_a,
    buf_b,
    buf_c,
    halves_b,
    halves_c,
    products,
    mixed,
    send_sem,
    recv_sem,
    sum_send,
    sum_recv,
):
    ny, nx = sizes
    gy, gx = lax.axis_index("gy"), lax.axis_index("gx")

    def at(dy, dx):
        return (lax.rem(gy + (dy % ny), ny), lax.rem(gx + (dx % nx), nx))

    peers = {(dy % ny, dx % nx) for dy in range(-2, 3) for dx in range(-1, 2)}
    peers |= {(d, 0) for d in range(ny)} | {(0, d) for d in range(nx)}
    peers = sorted(peers - {(0, 0)})
    barrier = pltpu.get_barrier_semaphore()
    for dy, dx in peers:
        pl.semaphore_signal(barrier, inc=1, device_id=at(dy, dx), device_id_type=MESH)

    inputs = [
        pltpu.make_async_copy(source, target, input_sem.at[i])
        for i, (source, target) in enumerate(
            (
                (mask_hbm, mask_ref),
                (target_hbm, target_ref),
                (kernels_hbm, kernels_ref),
                (offsets_hbm, offsets_ref),
                (weights_hbm, weights_ref),
            )
        )
    ]
    for copy in inputs:
        copy.start()
    inputs[0].wait()
    inputs[1].wait()

    own_plane = mask_ref[...].astype(BF16).astype(F32)
    own_target = target_ref[...].astype(F32)
    lane = lane_index(ROWS, 128)
    whole[0] = own_plane.astype(BF16)
    whole[1] = own_target.astype(BF16)
    left = jnp.where(lane < 64, own_plane, pltpu.roll(own_target, 64, 1))
    right = jnp.where(lane < 64, pltpu.roll(own_plane, 54, 1), pltpu.roll(own_target, 91, 1))
    edges[0] = left.astype(BF16)
    edges[1] = right.astype(BF16)
    for i, value in enumerate((right, own_plane, left)):
        rims[i, 0] = value[24:40, :].astype(BF16)
        rims[i, 1] = value[0:16, :].astype(BF16)

    inputs[2].wait()
    build_taps(kernels_ref, taps32, taps)

    pl.semaphore_wait(barrier, len(peers))

    copies = []

    def send(source, target, dy, dx):
        slot = len(copies)
        copies.append(
            pltpu.make_async_remote_copy(
                src_ref=source,
                dst_ref=target,
                send_sem=send_sem.at[slot],
                recv_sem=recv_sem.at[slot],
                device_id=at(dy, dx),
                device_id_type=MESH,
            )
        )
        copies[-1].start()

    for dx in (1, -1):
        side = 1 if dx == 1 else 0
        for dy in (-1, 0, 1):
            send(edges.at[side], got_edges.at[0 if dx == 1 else 1, 1 - dy], dy, dx)
    for dx in (1, -1, 0):
        for dy in (2, -2):
            end = 0 if dy == 2 else 1
            send(rims.at[1 - dx, end], got_rims.at[1 - dx, end], dy, dx)
    for dy in (1, -1):
        send(whole, got_whole.at[0 if dy == 1 else 1], dy, 0)
    build_mixer(taps32, mixer32, mixer)
    inputs[3].wait()
    inputs[4].wait()
    for ref in (buf_a, buf_b, buf_c):
        ref[0:8, :] = jnp.zeros((8, LANES), F32)
        ref[8 + BANDS * BAND :, :] = jnp.zeros((8, LANES), F32)
    patches[152 * PITCH :, :] = jnp.zeros((96, LANES), BF16)
    for copy in copies:
        copy.wait()

    first_row = gy * ROWS
    first_col = gx * COLS
    total_rows, total_cols = ny * ROWS, nx * COLS

    def framed(row, rows, middle, west, east):
        n = lane_index(rows, 128)
        moved = pltpu.roll(middle, PLANE_MARGIN, 1)
        low = jnp.where(n < PLANE_MARGIN, west, moved)
        high = jnp.where(n < PLANE_MARGIN, moved, jnp.where(n < 2 * PLANE_MARGIN, pltpu.roll(east, 54, 1), 0.0))
        value = jnp.concatenate([low, high], axis=1)
        y = first_row - PLANE_MARGIN - 2 + row + row_index(rows)
        x = first_col - PLANE_MARGIN + lane_index(rows)
        inside = (y >= 0) & (y < total_rows) & (x >= 0) & (x < total_cols)
        plane[row : row + rows, :] = pltpu.roll(jnp.where(inside, value, 0.0), LANES - TAPS + 1 - 4, 1)

    def wide(value):
        return value.astype(F32)

    framed(0, 16, wide(got_rims[1, 0]), wide(got_rims[0, 0]), wide(got_rims[2, 0]))
    framed(16, 40, wide(got_whole[0, 0]), wide(got_edges[0, 0]), wide(got_edges[1, 0]))
    framed(56, 40, own_plane, wide(got_edges[0, 1]), wide(got_edges[1, 1]))
    framed(96, 40, wide(got_whole[1, 0]), wide(got_edges[0, 2]), wide(got_edges[1, 2]))
    framed(136, 16, wide(got_rims[1, 1]), wide(got_rims[0, 1]), wide(got_rims[2, 1]))
    plane[152:160, :] = jnp.zeros((8, LANES), F32)

    def framed_target(row, middle, west, east):
        n = lane_index(ROWS, 128)
        moved = pltpu.roll(middle, FIELD_MARGIN, 1)
        wanted[row : row + ROWS, 0:128] = jnp.where(n < FIELD_MARGIN, pltpu.roll(west, 74, 1), moved)
        wanted[row : row + ROWS, 128:256] = jnp.where(n < FIELD_MARGIN, moved, pltpu.roll(east, 101, 1))

    framed_target(0, wide(got_whole[0, 1]), wide(got_edges[0, 0]), wide(got_edges[1, 0]))
    framed_target(40, own_target, wide(got_edges[0, 1]), wide(got_edges[1, 1]))
    framed_target(80, wide(got_whole[1, 1]), wide(got_edges[0, 2]), wide(got_edges[1, 2]))

    n8 = row_index(8)

    def spread(chunk):
        for v in range(chunk * 8, chunk * 8 + 8, 4):
            pieces = []
            for u in (v, v + 2):
                even = jnp.broadcast_to(plane[u + 2 : u + 3, :], (40, LANES))
                odd = jnp.broadcast_to(plane[u + 3 : u + 4, :], (40, LANES))
                even = pltpu.roll(even, 4, 1, stride=1, stride_axis=0)
                odd = pltpu.roll(odd, 0, 1, stride=1, stride_axis=0)
                pieces += [even[0:32], jnp.where(n8 < 4, even[32:40], odd[0:8]), odd[8:40]]
            patches[v * PITCH : (v + 4) * PITCH, :] = jnp.concatenate(pieces, axis=0).astype(BF16)

    for chunk in range(6):
        spread(chunk)

    def inside_field(start, rows):
        y = first_row - FIELD_MARGIN + start + row_index(rows)
        x = first_col - FIELD_MARGIN + lane_index(rows)
        return (y >= 0) & (y < total_rows) & (x >= 0) & (x < total_cols)

    def band(i):
        first = i * BAND * PITCH
        value = jnp.dot(taps[...], patches[first : first + DEPTH, :], preferred_element_type=F32)
        value = value.reshape(CHANNELS, BAND, LANES)
        start = i * BAND
        if FIRST_BAND <= i <= LAST_BAND:
            field[:, start : start + BAND, :] = value
        intensity = jnp.sum(value * value, axis=0) / KERNELS
        buf_a[start + 8 : start + 8 + BAND, :] = jnp.where(inside_field(start, BAND), intensity, 0.0)

    for i in range(BANDS):
        if i + 6 < 19:
            spread(i + 6)
        band(i)

    dense = smooth(buf_a, 8, 120)
    develop = jnp.where(inside_field(0, 120), jax.nn.sigmoid(SHARPNESS * (dense - THRESHOLD)), 0.0)
    buf_b[8:128, :] = develop
    for i in range(2):
        halves_b[i, 8:128, :] = develop[:, i * 128 : (i + 1) * 128]
        halves_b[i, 0:8, :] = jnp.zeros((8, 128), F32)
        halves_b[i, 128:136, :] = jnp.zeros((8, 128), F32)

    loading = jnp.zeros((104, LANES), F32)
    for j in range(LOAD_TAPS):
        part = rows_from(halves_b, 16 + offsets_ref[0, j], 104)
        loading = loading + weights_ref[j] * pltpu.roll(part, lax.rem(LANES - offsets_ref[1, j], LANES), 1)
    printed = buf_b[16:120, :] - LOADING_GAIN / LOAD_TAPS * loading
    y = first_row - FIELD_MARGIN + 8 + row_index(104)
    x = first_col - FIELD_MARGIN + lane_index(104)
    weight = (1.0 + 2.0 * y.astype(F32) / total_rows) * (1.0 + 2.0 * x.astype(F32) / total_cols)
    diff = printed - wanted[11:115, :]
    own = (y >= first_row) & (y < first_row + ROWS) & (x >= first_col) & (x < first_col + COLS)
    loss = jnp.sum(jnp.where(own, weight * diff * diff, 0.0), axis=0, keepdims=True)
    resid = jnp.where(inside_field(8, 104), 2.0 * weight * diff, 0.0)
    buf_c[16:120, :] = resid
    for i in range(2):
        halves_c[i, 16:120, :] = resid[:, i * 128 : (i + 1) * 128]

    back = jnp.zeros((88, LANES), F32)
    for j in range(LOAD_TAPS):
        part = rows_from(halves_c, 24 - offsets_ref[0, j], 88)
        back = back + weights_ref[j] * pltpu.roll(part, lax.rem(LANES + offsets_ref[1, j], LANES), 1)
    slope = buf_c[24:112, :] - LOADING_GAIN / LOAD_TAPS * back
    nearby = buf_b[24:112, :]
    buf_a[24:112, :] = slope * SHARPNESS * nearby * (1.0 - nearby)
    pull = smooth(buf_a, 24, 80)
    buf_b[24:104, :] = jnp.where(inside_field(16, 80), pull, 0.0)

    def weigh(i, carry):
        start = pl.multiple_of((i + FIRST_BAND) * BAND, BAND)
        value = 2.0 * field[:, pl.ds(start, BAND), :] * buf_b[pl.ds(start + 8, BAND), :][None] / KERNELS
        rows = pl.ds(pl.multiple_of(i * CHANNELS * BAND, CHANNELS * BAND), CHANNELS * BAND)
        products[rows, :] = value.reshape(CHANNELS * BAND, LANES).astype(BF16)
        return carry

    lax.fori_loop(0, LAST_BAND - FIRST_BAND + 1, weigh, 0)

    def mix(g, carry):
        rows = pl.ds(pl.multiple_of(g * CHANNELS * BAND, CHANNELS * BAND), 6 * CHANNELS * BAND)
        value = jnp.dot(mixer[...], products[rows, :], preferred_element_type=F32)
        for i in range(2):
            mixed[i, pl.ds(pl.multiple_of(g * 8 * PITCH, 8 * PITCH), 8 * PITCH), :] = value[:, i * 128 : (i + 1) * 128]
        return carry

    lax.fori_loop(0, ROWS // 8, mix, 0)

    gradient = jnp.zeros((ROWS, 128), F32)
    for t in range(TAPS):
        part = jnp.concatenate([mixed[i, pl.ds(t, ROWS, stride=PITCH), :] for i in range(2)], axis=1)
        gradient = gradient + pltpu.roll(part, 236 - t, 1)[:, 0:128]

    def gather(sums, axis_size, me, number):
        out = []
        for d in range(1, axis_size):
            peer = lax.rem(me + d, axis_size)
            out.append(
                pltpu.make_async_remote_copy(
                    src_ref=sums.at[me],
                    dst_ref=sums.at[me],
                    send_sem=sum_send.at[number, d],
                    recv_sem=sum_recv.at[number, d],
                    device_id=(peer, gx) if number == 0 else (gy, peer),
                    device_id_type=MESH,
                )
            )
            out[-1].start()
        for copy in out:
            copy.wait()

    square = jnp.sum(gradient * gradient, axis=0, keepdims=True)
    sums_y[gy, 0:1, :] = loss[:, 0:128] + loss[:, 128:256]
    sums_y[gy, 1:2, :] = square
    gather(sums_y, ny, gy, 0)
    sums_x[gx] = jnp.sum(sums_y[...], axis=0)
    gather(sums_x, nx, gx, 1)
    totals = jnp.sum(jnp.sum(sums_x[...], axis=0), axis=1, keepdims=True)
    loss_ref[...] = totals[0:1, :]
    scale = jnp.sqrt(totals[1:2, :] / (total_rows * total_cols) + 1e-06)
    update_ref[...] = mask_ref[...] - gradient / scale


def solution(mesh):
    ny, nx = mesh.shape["gy"], mesh.shape["gx"]
    vmem = pl.BlockSpec(memory_space=pltpu.VMEM)
    rows = CHANNELS * BAND

    def step(mask, target, kernels, offsets, load_weights):
        update, loss = pl.pallas_call(
            functools.partial(kernel, (ny, nx)),
            out_shape=(
                jax.ShapeDtypeStruct((ROWS, COLS), F32),
                jax.ShapeDtypeStruct((1, 1), F32),
            ),
            in_specs=[pl.BlockSpec(memory_space=pl.ANY)] * 5,
            out_specs=(vmem, vmem),
            scratch_shapes=[
                pltpu.SMEM((2, LOAD_TAPS), jnp.int32),
                pltpu.SMEM((LOAD_TAPS,), F32),
                pltpu.VMEM((ROWS, COLS), F32),
                pltpu.VMEM((ROWS, COLS), jnp.int32),
                pltpu.VMEM((TAPS, CHANNELS, TAPS), BF16),
                pltpu.SemaphoreType.DMA((5,)),
                pltpu.VMEM((2, ROWS, COLS), BF16),
                pltpu.VMEM((2, ROWS, COLS), BF16),
                pltpu.VMEM((3, 2, 16, COLS), BF16),
                pltpu.VMEM((2, 2, ROWS, COLS), BF16),
                pltpu.VMEM((2, 3, ROWS, COLS), BF16),
                pltpu.VMEM((3, 2, 16, COLS), BF16),
                pltpu.VMEM((ny, 2, 128), F32),
                pltpu.VMEM((nx, 2, 128), F32),
                pltpu.VMEM((DEPTH // 128, rows, 128), F32),
                pltpu.VMEM((rows, DEPTH), BF16),
                pltpu.VMEM((6 * rows, 384), F32),
                pltpu.VMEM((8 * PITCH, 6 * rows), BF16),
                pltpu.VMEM((160, LANES), F32),
                pltpu.VMEM((120, LANES), F32),
                pltpu.VMEM((152 * PITCH + 96, LANES), BF16),
                pltpu.VMEM((CHANNELS, BANDS * BAND, LANES), F32),
                pltpu.VMEM((136, LANES), F32),
                pltpu.VMEM((136, LANES), F32),
                pltpu.VMEM((136, LANES), F32),
                pltpu.VMEM((2, 136, 128), F32),
                pltpu.VMEM((2, 136, 128), F32),
                pltpu.VMEM((10 * rows, LANES), BF16),
                pltpu.VMEM((2, ROWS * PITCH, 128), F32),
                pltpu.SemaphoreType.DMA((14,)),
                pltpu.SemaphoreType.DMA((14,)),
                pltpu.SemaphoreType.DMA((2, 32)),
                pltpu.SemaphoreType.DMA((2, 32)),
            ],
            compiler_params=pltpu.CompilerParams(collective_id=0, has_side_effects=True),
        )(offsets.T, load_weights, mask, target, kernels.transpose(1, 0, 2))
        return update, loss[0, 0]

    placed = (P("gy", "gx"), P("gy", "gx"), P(), P(), P())
    return jax.shard_map(step, mesh=mesh, in_specs=placed, out_specs=(P("gy", "gx"), P()), check_vma=False)
```

```python
import functools

import jax
import jax.numpy as jnp
from jax import lax
from jax.experimental import pallas as pl
from jax.experimental.pallas import tpu as pltpu
from jax.sharding import PartitionSpec as P

MESH = pl.DeviceIdType.MESH
F32 = jnp.float32
BF16 = jnp.bfloat16

KERNELS = 12
CHANNELS = 24
TAPS = 35
REACH = 8
LOAD_TAPS = 8
SMOOTH_TAPS = (0.0625, 0.25, 0.375, 0.25, 0.0625)
SHARPNESS = 4.0
THRESHOLD = 0.65
LOADING_GAIN = 0.5

ROWS, COLS = 40, 128
LANES = 256
FIELD_MARGIN = 37
PLANE_MARGIN = 54
PITCH = 36
BAND = 8
DEPTH = 1536
BANDS = 15
FIRST_BAND, LAST_BAND = 2, 11


def lane_index(rows, lanes=LANES):
    return lax.broadcasted_iota(jnp.int32, (rows, lanes), 1)


def row_index(rows, lanes=LANES):
    return lax.broadcasted_iota(jnp.int32, (rows, lanes), 0)


def smooth(ref, start, rows):
    down = sum(SMOOTH_TAPS[a] * ref[pl.ds(start + a - 2, rows), :] for a in range(5))
    total = SMOOTH_TAPS[2] * down
    for b in (0, 1, 3, 4):
        total = total + SMOOTH_TAPS[b] * pltpu.roll(down, (2 - b) % LANES, 1)
    return total


def rows_from(halves, start, rows):
    return jnp.concatenate([halves[i, pl.ds(start, rows), :] for i in range(2)], axis=1)


def build_taps(kernels_ref, taps32, taps):
    flip = (
        lax.broadcasted_iota(jnp.int32, (TAPS, 128), 0) + lax.broadcasted_iota(jnp.int32, (TAPS, 128), 1) == TAPS - 1
    ).astype(BF16)
    lane = lane_index(CHANNELS, 128)
    tiles = [jnp.zeros((CHANNELS, 128), F32) for _ in range(DEPTH // 128)]
    for a in range(TAPS):
        tile, shift = divmod(a * PITCH, 128)
        row = jnp.dot(kernels_ref[a], flip, preferred_element_type=F32)
        moved = pltpu.roll(row, shift, 1) if shift else row
        tiles[tile] = tiles[tile] + jnp.where(lane >= shift, moved, 0.0)
        if shift + TAPS > 128:
            tiles[tile + 1] = tiles[tile + 1] + jnp.where(lane < shift, moved, 0.0)
    base = jnp.concatenate(tiles, axis=1)
    for y in range(BAND):
        moved = pltpu.roll(base, y * PITCH, 1) if y else base
        for i in range(DEPTH // 128):
            taps32[i, pl.ds(y, CHANNELS, stride=BAND), :] = moved[:, i * 128 : (i + 1) * 128]
    for i in range(DEPTH // 128):
        taps[:, i * 128 : (i + 1) * 128] = taps32[i].astype(BF16)


def build_mixer(taps32, mixer32, mixer):
    joined = jnp.concatenate([taps32[i] for i in range(DEPTH // 128)], axis=1)
    rows = CHANNELS * BAND
    for n in range(6):
        first = (PLANE_MARGIN - 8 * (n + 2)) * PITCH
        low, high = max(first, 0), min(first + 8 * PITCH, DEPTH)
        window = joined[:, low:high]
        if first < 0:
            window = jnp.concatenate([jnp.zeros((rows, -first), F32), window], axis=1)
        if high < first + 8 * PITCH:
            window = jnp.concatenate([window, jnp.zeros((rows, first + 8 * PITCH - high), F32)], axis=1)
        mixer32[n * rows : (n + 1) * rows, 0 : 8 * PITCH] = window
    mixer[...] = mixer32[...].T[0 : 8 * PITCH, :].astype(BF16)


def kernel(
    sizes,
    offsets_hbm,
    weights_hbm,
    mask_hbm,
    target_hbm,
    kernels_hbm,
    gradient_hbm,
    sums_ref,
    offsets_ref,
    weights_ref,
    mask_ref,
    target_ref,
    kernels_ref,
    gradient_ref,
    input_sem,
    whole,
    edges,
    rims,
    got_whole,
    got_edges,
    got_rims,
    sums_y,
    sums_x,
    taps32,
    taps,
    mixer32,
    mixer,
    plane,
    wanted,
    patches,
    field,
    buf_a,
    buf_b,
    buf_c,
    halves_b,
    halves_c,
    products,
    mixed,
    send_sem,
    recv_sem,
    sum_send,
    sum_recv,
    known,
):
    ny, nx = sizes
    gy, gx = lax.axis_index("gy"), lax.axis_index("gx")

    def at(dy, dx):
        return (lax.rem(gy + (dy % ny), ny), lax.rem(gx + (dx % nx), nx))

    inputs = [
        pltpu.make_async_copy(source, target, input_sem.at[i])
        for i, (source, target) in enumerate(
            (
                (mask_hbm, mask_ref),
                (target_hbm, target_ref),
                (kernels_hbm, kernels_ref),
                (offsets_hbm, offsets_ref),
                (weights_hbm, weights_ref),
            )
        )
    ]
    for copy in inputs:
        copy.start()
    peers = sorted({(dy % ny, dx % nx) for dy in range(-2, 3) for dx in range(-1, 2)} - {(0, 0)})
    barrier = pltpu.get_barrier_semaphore()
    for dy, dx in peers:
        pl.semaphore_signal(barrier, inc=1, device_id=at(dy, dx), device_id_type=MESH)

    rounds_y = [r for r in (2, 4, 8) if 2 * r < ny]
    rounds_x = [r for r in (1, 2, 4, 8) if 2 * r < nx]

    def tell(number):
        for along_x, rounds in ((0, rounds_y), (1, rounds_x)):
            if number < len(rounds):
                for r in (rounds[number], -rounds[number]):
                    pl.semaphore_signal(
                        known.at[along_x, number],
                        inc=1,
                        device_id=at(0, r) if along_x else at(r, 0),
                        device_id_type=MESH,
                    )

    def learn(number):
        for along_x, rounds in ((0, rounds_y), (1, rounds_x)):
            if number < len(rounds):
                pl.semaphore_wait(known.at[along_x, number], 2)

    inputs[0].wait()
    inputs[1].wait()

    own_plane = mask_ref[...].astype(BF16).astype(F32)
    own_target = target_ref[...].astype(F32)
    lane = lane_index(ROWS, 128)
    whole[0] = own_plane.astype(BF16)
    whole[1] = own_target.astype(BF16)
    left = jnp.where(lane < 64, own_plane, pltpu.roll(own_target, 64, 1))
    right = jnp.where(lane < 64, pltpu.roll(own_plane, 54, 1), pltpu.roll(own_target, 91, 1))
    edges[0] = left.astype(BF16)
    edges[1] = right.astype(BF16)
    for i, value in enumerate((right, own_plane, left)):
        rims[i, 0] = value[24:40, :].astype(BF16)
        rims[i, 1] = value[0:16, :].astype(BF16)

    pl.semaphore_wait(barrier, len(peers))

    def send(kind, source, target, dy, dx):
        pltpu.make_async_remote_copy(
            src_ref=source,
            dst_ref=target,
            send_sem=send_sem.at[kind],
            recv_sem=recv_sem.at[kind],
            device_id=at(dy, dx),
            device_id_type=MESH,
        ).start()

    def wait_all(ref, sent, received):
        for sem in (sent, received):
            pltpu.make_async_copy(ref, ref, sem).wait()

    for dx in (1, -1):
        side = 1 if dx == 1 else 0
        for dy in (-1, 0, 1):
            send(0, edges.at[side], got_edges.at[0 if dx == 1 else 1, 1 - dy], dy, dx)
    for dx in (1, -1, 0):
        for dy in (2, -2):
            end = 0 if dy == 2 else 1
            send(1, rims.at[1 - dx, end], got_rims.at[1 - dx, end], dy, dx)
    for dy in (1, -1):
        send(2, whole, got_whole.at[0 if dy == 1 else 1], dy, 0)
    tell(0)
    inputs[2].wait()
    build_taps(kernels_ref, taps32, taps)
    learn(0)
    tell(1)
    build_mixer(taps32, mixer32, mixer)
    learn(1)
    tell(2)
    inputs[3].wait()
    inputs[4].wait()
    for ref in (buf_a, buf_b, buf_c):
        ref[0:8, :] = jnp.zeros((8, LANES), F32)
        ref[8 + BANDS * BAND :, :] = jnp.zeros((8, LANES), F32)
    patches[152 * PITCH :, :] = jnp.zeros((96, LANES), BF16)
    for kind, ref in enumerate((got_edges, got_rims, got_whole)):
        wait_all(ref, send_sem.at[kind], recv_sem.at[kind])

    first_row = gy * ROWS
    first_col = gx * COLS
    total_rows, total_cols = ny * ROWS, nx * COLS

    def framed(row, rows, middle, west, east):
        n = lane_index(rows, 128)
        moved = pltpu.roll(middle, PLANE_MARGIN, 1)
        low = jnp.where(n < PLANE_MARGIN, west, moved)
        high = jnp.where(n < PLANE_MARGIN, moved, jnp.where(n < 2 * PLANE_MARGIN, pltpu.roll(east, 54, 1), 0.0))
        value = jnp.concatenate([low, high], axis=1)
        y = first_row - PLANE_MARGIN - 2 + row + row_index(rows)
        x = first_col - PLANE_MARGIN + lane_index(rows)
        inside = (y >= 0) & (y < total_rows) & (x >= 0) & (x < total_cols)
        plane[row : row + rows, :] = pltpu.roll(jnp.where(inside, value, 0.0), LANES - TAPS + 1 - 4, 1)

    def wide(value):
        return value.astype(F32)

    framed(0, 16, wide(got_rims[1, 0]), wide(got_rims[0, 0]), wide(got_rims[2, 0]))
    framed(16, 40, wide(got_whole[0, 0]), wide(got_edges[0, 0]), wide(got_edges[1, 0]))
    framed(56, 40, own_plane, wide(got_edges[0, 1]), wide(got_edges[1, 1]))
    framed(96, 40, wide(got_whole[1, 0]), wide(got_edges[0, 2]), wide(got_edges[1, 2]))
    framed(136, 16, wide(got_rims[1, 1]), wide(got_rims[0, 1]), wide(got_rims[2, 1]))
    plane[152:160, :] = jnp.zeros((8, LANES), F32)

    def framed_target(row, middle, west, east):
        n = lane_index(ROWS, 128)
        moved = pltpu.roll(middle, FIELD_MARGIN, 1)
        wanted[row : row + ROWS, 0:128] = jnp.where(n < FIELD_MARGIN, pltpu.roll(west, 74, 1), moved)
        wanted[row : row + ROWS, 128:256] = jnp.where(n < FIELD_MARGIN, moved, pltpu.roll(east, 101, 1))

    framed_target(0, wide(got_whole[0, 1]), wide(got_edges[0, 0]), wide(got_edges[1, 0]))
    framed_target(40, own_target, wide(got_edges[0, 1]), wide(got_edges[1, 1]))
    framed_target(80, wide(got_whole[1, 1]), wide(got_edges[0, 2]), wide(got_edges[1, 2]))

    n8 = row_index(8)

    def spread(chunk):
        for v in range(chunk * 8, chunk * 8 + 8, 4):
            pieces = []
            for u in (v, v + 2):
                even = jnp.broadcast_to(plane[u + 2 : u + 3, :], (40, LANES))
                odd = jnp.broadcast_to(plane[u + 3 : u + 4, :], (40, LANES))
                even = pltpu.roll(even, 4, 1, stride=1, stride_axis=0)
                odd = pltpu.roll(odd, 0, 1, stride=1, stride_axis=0)
                pieces += [even[0:32], jnp.where(n8 < 4, even[32:40], odd[0:8]), odd[8:40]]
            patches[v * PITCH : (v + 4) * PITCH, :] = jnp.concatenate(pieces, axis=0).astype(BF16)

    for chunk in range(6):
        spread(chunk)

    def inside_field(start, rows):
        y = first_row - FIELD_MARGIN + start + row_index(rows)
        x = first_col - FIELD_MARGIN + lane_index(rows)
        return (y >= 0) & (y < total_rows) & (x >= 0) & (x < total_cols)

    def band(i):
        first = i * BAND * PITCH
        value = jnp.dot(taps[...], patches[first : first + DEPTH, :], preferred_element_type=F32)
        value = value.reshape(CHANNELS, BAND, LANES)
        start = i * BAND
        if FIRST_BAND <= i <= LAST_BAND:
            field[:, start : start + BAND, :] = value
        intensity = jnp.sum(value * value, axis=0) / KERNELS
        buf_a[start + 8 : start + 8 + BAND, :] = jnp.where(inside_field(start, BAND), intensity, 0.0)

    for i in range(BANDS):
        if i + 6 < 19:
            spread(i + 6)
        band(i)
        if i == 9:
            learn(2)
            tell(3)

    dense = smooth(buf_a, 8, 120)
    develop = jnp.where(inside_field(0, 120), jax.nn.sigmoid(SHARPNESS * (dense - THRESHOLD)), 0.0)
    buf_b[8:128, :] = develop
    for i in range(2):
        halves_b[i, 8:128, :] = develop[:, i * 128 : (i + 1) * 128]
        halves_b[i, 0:8, :] = jnp.zeros((8, 128), F32)
        halves_b[i, 128:136, :] = jnp.zeros((8, 128), F32)

    loading = jnp.zeros((104, LANES), F32)
    for j in range(LOAD_TAPS):
        part = rows_from(halves_b, 16 + offsets_ref[0, j], 104)
        loading = loading + weights_ref[j] * pltpu.roll(part, lax.rem(LANES - offsets_ref[1, j], LANES), 1)
    printed = buf_b[16:120, :] - LOADING_GAIN / LOAD_TAPS * loading
    y = first_row - FIELD_MARGIN + 8 + row_index(104)
    x = first_col - FIELD_MARGIN + lane_index(104)
    weight = (1.0 + 2.0 * y.astype(F32) / total_rows) * (1.0 + 2.0 * x.astype(F32) / total_cols)
    diff = printed - wanted[11:115, :]
    own = (y >= first_row) & (y < first_row + ROWS) & (x >= first_col) & (x < first_col + COLS)
    loss = jnp.sum(jnp.where(own, weight * diff * diff, 0.0), axis=0, keepdims=True)
    resid = jnp.where(inside_field(8, 104), 2.0 * weight * diff, 0.0)
    buf_c[16:120, :] = resid
    for i in range(2):
        halves_c[i, 16:120, :] = resid[:, i * 128 : (i + 1) * 128]

    back = jnp.zeros((88, LANES), F32)
    for j in range(LOAD_TAPS):
        part = rows_from(halves_c, 24 - offsets_ref[0, j], 88)
        back = back + weights_ref[j] * pltpu.roll(part, lax.rem(LANES + offsets_ref[1, j], LANES), 1)
    slope = buf_c[24:112, :] - LOADING_GAIN / LOAD_TAPS * back
    nearby = buf_b[24:112, :]
    buf_a[24:112, :] = slope * SHARPNESS * nearby * (1.0 - nearby)
    pull = smooth(buf_a, 24, 80)
    buf_b[24:104, :] = jnp.where(inside_field(16, 80), pull, 0.0)

    def weigh(i):
        start = (i + FIRST_BAND) * BAND
        value = 2.0 * field[:, start : start + BAND, :] * buf_b[start + 8 : start + 8 + BAND, :][None] / KERNELS
        rows = CHANNELS * BAND
        products[i * rows : (i + 1) * rows, :] = value.reshape(rows, LANES).astype(BF16)

    def mix(g):
        rows = CHANNELS * BAND
        value = jnp.dot(mixer[...], products[g * rows : (g + 6) * rows, :], preferred_element_type=F32)
        for i in range(2):
            mixed[i, g * 8 * PITCH : (g + 1) * 8 * PITCH, :] = value[:, i * 128 : (i + 1) * 128]

    def gather_taps(g):
        total = jnp.zeros((8, LANES), F32)
        for t in range(TAPS):
            rows = pl.ds(g * 8 * PITCH + t, 8, stride=PITCH)
            part = jnp.concatenate([mixed[i, rows, :] for i in range(2)], axis=1)
            total = total + pltpu.roll(part, 236 - t, 1)
        return total[:, 0:128]

    for i in range(5):
        weigh(i)
    parts = []
    for g in range(ROWS // 8):
        weigh(g + 5)
        mix(g)
        if g:
            parts.append(gather_taps(g - 1))
    parts.append(gather_taps(ROWS // 8 - 1))
    gradient = jnp.concatenate(parts, axis=0)

    inner = max(d for d in (1, 2, 4) if nx % d == 0)
    outer = nx // inner

    def ring(d, n):
        return min(d, n - d)

    def gather(sums, number):
        if number == 0:
            hops = [(ring(d, ny), d, 0) for d in range(1, ny)]
        else:
            hops = [(ring(a, outer) + ring(b, inner), a, b) for a in range(outer) for b in range(inner) if a or b]
        me = gx if number else gy
        for _, a, b in sorted(hops, reverse=True):
            if number == 0:
                device = at(a, 0)
            else:
                y, x = lax.rem(gx // inner + a, outer), lax.rem(lax.rem(gx, inner) + b, inner)
                device = (gy, y * inner + x)
            pltpu.make_async_remote_copy(
                src_ref=sums.at[me],
                dst_ref=sums.at[me],
                send_sem=sum_send.at[number],
                recv_sem=sum_recv.at[number],
                device_id=device,
                device_id_type=MESH,
            ).start()
        wait_all(sums.at[pl.ds(0, len(hops))], sum_send.at[number], sum_recv.at[number])

    gradient_ref[...] = gradient
    out = pltpu.make_async_copy(gradient_ref, gradient_hbm, input_sem.at[5])
    out.start()
    square = jnp.sum(gradient * gradient, axis=0, keepdims=True)
    sums_y[gy, 0:1, :] = loss[:, 0:128] + loss[:, 128:256]
    sums_y[gy, 1:2, :] = square
    gather(sums_y, 0)
    learn(3)
    sums_x[gx] = jnp.sum(sums_y[...], axis=0)
    gather(sums_x, 1)
    sums_ref[...] = jnp.sum(sums_x[...], axis=0)
    out.wait()


def finish(pixels, mask_ref, gradient_ref, sums_ref, update_ref, loss_ref):
    totals = jnp.sum(sums_ref[...], axis=1, keepdims=True)
    loss_ref[...] = totals[0:1, :]
    scale = jnp.sqrt(totals[1:2, :] / pixels + 1e-06)
    update_ref[...] = mask_ref[...] - gradient_ref[...] / scale


def solution(mesh):
    ny, nx = mesh.shape["gy"], mesh.shape["gx"]
    vmem = pl.BlockSpec(memory_space=pltpu.VMEM)
    rows = CHANNELS * BAND

    def step(mask, target, kernels, offsets, load_weights):
        gradient, sums = pl.pallas_call(
            functools.partial(kernel, (ny, nx)),
            out_shape=(
                jax.ShapeDtypeStruct((ROWS, COLS), F32),
                jax.ShapeDtypeStruct((2, 128), F32),
            ),
            in_specs=[pl.BlockSpec(memory_space=pl.ANY)] * 5,
            out_specs=(pl.BlockSpec(memory_space=pl.ANY), vmem),
            scratch_shapes=[
                pltpu.SMEM((2, LOAD_TAPS), jnp.int32),
                pltpu.SMEM((LOAD_TAPS,), F32),
                pltpu.VMEM((ROWS, COLS), F32),
                pltpu.VMEM((ROWS, COLS), jnp.int32),
                pltpu.VMEM((TAPS, CHANNELS, TAPS), BF16),
                pltpu.VMEM((ROWS, COLS), F32),
                pltpu.SemaphoreType.DMA((6,)),
                pltpu.VMEM((2, ROWS, COLS), BF16),
                pltpu.VMEM((2, ROWS, COLS), BF16),
                pltpu.VMEM((3, 2, 16, COLS), BF16),
                pltpu.VMEM((2, 2, ROWS, COLS), BF16),
                pltpu.VMEM((2, 3, ROWS, COLS), BF16),
                pltpu.VMEM((3, 2, 16, COLS), BF16),
                pltpu.VMEM((ny, 2, 128), F32),
                pltpu.VMEM((nx, 2, 128), F32),
                pltpu.VMEM((DEPTH // 128, rows, 128), F32),
                pltpu.VMEM((rows, DEPTH), BF16),
                pltpu.VMEM((6 * rows, 384), F32),
                pltpu.VMEM((8 * PITCH, 6 * rows), BF16),
                pltpu.VMEM((160, LANES), F32),
                pltpu.VMEM((120, LANES), F32),
                pltpu.VMEM((152 * PITCH + 96, LANES), BF16),
                pltpu.VMEM((CHANNELS, BANDS * BAND, LANES), F32),
                pltpu.VMEM((136, LANES), F32),
                pltpu.VMEM((136, LANES), F32),
                pltpu.VMEM((136, LANES), F32),
                pltpu.VMEM((2, 136, 128), F32),
                pltpu.VMEM((2, 136, 128), F32),
                pltpu.VMEM((10 * rows, LANES), BF16),
                pltpu.VMEM((2, ROWS * PITCH, 128), F32),
                pltpu.SemaphoreType.DMA((3,)),
                pltpu.SemaphoreType.DMA((3,)),
                pltpu.SemaphoreType.DMA((2,)),
                pltpu.SemaphoreType.DMA((2,)),
                pltpu.SemaphoreType.REGULAR((2, 4)),
            ],
            compiler_params=pltpu.CompilerParams(collective_id=0, has_side_effects=True),
        )(offsets.T, load_weights, mask, target, kernels.transpose(1, 0, 2))
        update, loss = pl.pallas_call(
            functools.partial(finish, ny * ROWS * nx * COLS),
            out_shape=(
                jax.ShapeDtypeStruct((ROWS, COLS), F32),
                jax.ShapeDtypeStruct((1, 1), F32),
            ),
            in_specs=[vmem] * 3,
            out_specs=(vmem, vmem),
        )(mask, gradient, sums)
        return update, loss[0, 0]

    placed = (P("gy", "gx"), P("gy", "gx"), P(), P(), P())
    return jax.shard_map(step, mesh=mesh, in_specs=placed, out_specs=(P("gy", "gx"), P()), check_vma=False)
```

```python
import functools

import jax
import jax.numpy as jnp
from jax import lax
from jax.experimental import pallas as pl
from jax.experimental.pallas import tpu as pltpu
from jax.sharding import PartitionSpec as P

MESH = pl.DeviceIdType.MESH
F32 = jnp.float32
BF16 = jnp.bfloat16

KERNELS = 12
CHANNELS = 24
TAPS = 35
REACH = 8
LOAD_TAPS = 8
SMOOTH_TAPS = (0.0625, 0.25, 0.375, 0.25, 0.0625)
SHARPNESS = 4.0
THRESHOLD = 0.65
LOADING_GAIN = 0.5

ROWS, COLS = 40, 128
LANES = 256
FIELD_MARGIN = 37
PLANE_MARGIN = 54
PITCH = 36
BAND = 8
DEPTH = 1536
BANDS = 15
FIRST_BAND, LAST_BAND = 2, 11


def lane_index(rows, lanes=LANES):
    return lax.broadcasted_iota(jnp.int32, (rows, lanes), 1)


def row_index(rows, lanes=LANES):
    return lax.broadcasted_iota(jnp.int32, (rows, lanes), 0)


def rows_from(halves, start, rows):
    return jnp.concatenate([halves[i, pl.ds(start, rows), :] for i in range(2)], axis=1)


def rows_to(halves, start, value):
    for i in range(2):
        halves[i, start : start + value.shape[0], :] = value[:, i * 128 : (i + 1) * 128]


def smooth(halves, start, rows):
    down = sum(SMOOTH_TAPS[a] * rows_from(halves, start + a - 2, rows) for a in range(5))
    total = SMOOTH_TAPS[2] * down
    for b in (0, 1, 3, 4):
        total = total + SMOOTH_TAPS[b] * pltpu.roll(down, (2 - b) % LANES, 1)
    return total


def build_taps(kernels_ref, taps32, taps):
    flip = (
        lax.broadcasted_iota(jnp.int32, (TAPS, 128), 0) + lax.broadcasted_iota(jnp.int32, (TAPS, 128), 1) == TAPS - 1
    ).astype(BF16)
    lane = lane_index(CHANNELS, 128)
    tiles = [jnp.zeros((CHANNELS, 128), F32) for _ in range(DEPTH // 128)]
    for a in range(TAPS):
        tile, shift = divmod(a * PITCH, 128)
        row = jnp.dot(kernels_ref[a], flip, preferred_element_type=F32)
        moved = pltpu.roll(row, shift, 1) if shift else row
        tiles[tile] = tiles[tile] + jnp.where(lane >= shift, moved, 0.0)
        if shift + TAPS > 128:
            tiles[tile + 1] = tiles[tile + 1] + jnp.where(lane < shift, moved, 0.0)
    base = jnp.concatenate(tiles, axis=1)
    for y in range(BAND):
        moved = pltpu.roll(base, y * PITCH, 1) if y else base
        for i in range(DEPTH // 128):
            taps32[i, pl.ds(y, CHANNELS, stride=BAND), :] = moved[:, i * 128 : (i + 1) * 128]
    for i in range(DEPTH // 128):
        taps[:, i * 128 : (i + 1) * 128] = taps32[i].astype(BF16)


def build_mixer(taps32, mixer32, mixer):
    joined = jnp.concatenate([taps32[i] for i in range(DEPTH // 128)], axis=1)
    rows = CHANNELS * BAND
    for n in range(6):
        first = (PLANE_MARGIN - 8 * (n + 2)) * PITCH
        low, high = max(first, 0), min(first + 8 * PITCH, DEPTH)
        window = joined[:, low:high]
        if first < 0:
            window = jnp.concatenate([jnp.zeros((rows, -first), F32), window], axis=1)
        if high < first + 8 * PITCH:
            window = jnp.concatenate([window, jnp.zeros((rows, first + 8 * PITCH - high), F32)], axis=1)
        mixer32[n * rows : (n + 1) * rows, 0 : 8 * PITCH] = window
    mixer[...] = mixer32[...].T[0 : 8 * PITCH, :].astype(BF16)


def kernel(
    sizes,
    offsets_hbm,
    weights_hbm,
    mask_hbm,
    target_hbm,
    kernels_hbm,
    mask_ref,
    gradient_ref,
    sums_ref,
    offsets_ref,
    weights_ref,
    target_ref,
    kernels_ref,
    input_sem,
    whole,
    edges,
    rims,
    got_whole,
    got_edges,
    got_rims,
    sums_y,
    sums_x,
    taps32,
    taps,
    mixer32,
    mixer,
    plane,
    wanted,
    patches,
    field,
    dim,
    lit,
    rest,
    pull,
    products,
    mixed,
    send_sem,
    recv_sem,
    sum_send,
    sum_recv,
    known,
):
    ny, nx = sizes
    gy, gx = lax.axis_index("gy"), lax.axis_index("gx")

    def at(dy, dx):
        return (lax.rem(gy + (dy % ny), ny), lax.rem(gx + (dx % nx), nx))

    inputs = [
        pltpu.make_async_copy(source, target, input_sem.at[i])
        for i, (source, target) in enumerate(
            (
                (mask_hbm, mask_ref),
                (target_hbm, target_ref),
                (kernels_hbm, kernels_ref),
                (offsets_hbm, offsets_ref),
                (weights_hbm, weights_ref),
            )
        )
    ]
    for copy in inputs:
        copy.start()
    peers = sorted({(dy % ny, dx % nx) for dy in range(-2, 3) for dx in range(-1, 2)} - {(0, 0)})
    barrier = pltpu.get_barrier_semaphore()
    for dy, dx in peers:
        pl.semaphore_signal(barrier, inc=1, device_id=at(dy, dx), device_id_type=MESH)

    rounds_y = [r for r in (2, 4, 8) if 2 * r < ny]
    rounds_x = [r for r in (1, 2, 4, 8) if 2 * r < nx]

    def tell(number):
        for along_x, rounds in ((0, rounds_y), (1, rounds_x)):
            if number < len(rounds):
                for r in (rounds[number], -rounds[number]):
                    pl.semaphore_signal(
                        known.at[along_x, number],
                        inc=1,
                        device_id=at(0, r) if along_x else at(r, 0),
                        device_id_type=MESH,
                    )

    def learn(number):
        for along_x, rounds in ((0, rounds_y), (1, rounds_x)):
            if number < len(rounds):
                pl.semaphore_wait(known.at[along_x, number], 2)

    inputs[0].wait()
    inputs[1].wait()

    own_plane = mask_ref[...].astype(BF16).astype(F32)
    own_target = target_ref[...].astype(F32)
    lane = lane_index(ROWS, 128)
    whole[0] = own_plane.astype(BF16)
    whole[1] = own_target.astype(BF16)
    left = jnp.where(lane < 64, own_plane, pltpu.roll(own_target, 64, 1))
    right = jnp.where(lane < 64, pltpu.roll(own_plane, 54, 1), pltpu.roll(own_target, 91, 1))
    edges[0] = left.astype(BF16)
    edges[1] = right.astype(BF16)
    for i, value in enumerate((right, own_plane, left)):
        rims[i, 0] = value[24:40, :].astype(BF16)
        rims[i, 1] = value[0:16, :].astype(BF16)

    pl.semaphore_wait(barrier, len(peers))

    def send(kind, source, target, dy, dx):
        pltpu.make_async_remote_copy(
            src_ref=source,
            dst_ref=target,
            send_sem=send_sem.at[kind],
            recv_sem=recv_sem.at[kind],
            device_id=at(dy, dx),
            device_id_type=MESH,
        ).start()

    def wait_all(ref, sent, received):
        for sem in (sent, received):
            pltpu.make_async_copy(ref, ref, sem).wait()

    for dx in (1, -1):
        side = 1 if dx == 1 else 0
        for dy in (-1, 0, 1):
            send(0, edges.at[side], got_edges.at[0 if dx == 1 else 1, 1 - dy], dy, dx)
    for dx in (1, -1, 0):
        for dy in (2, -2):
            end = 0 if dy == 2 else 1
            send(1, rims.at[1 - dx, end], got_rims.at[1 - dx, end], dy, dx)
    for dy in (1, -1):
        send(2, whole, got_whole.at[0 if dy == 1 else 1], dy, 0)
    tell(0)
    inputs[2].wait()
    build_taps(kernels_ref, taps32, taps)
    learn(0)
    tell(1)
    build_mixer(taps32, mixer32, mixer)
    learn(1)
    tell(2)
    inputs[3].wait()
    inputs[4].wait()
    rows_to(pull, 16, jnp.zeros((8, LANES), F32))
    patches[152 * PITCH :, :] = jnp.zeros((96, LANES), BF16)
    for kind, ref in enumerate((got_edges, got_rims, got_whole)):
        wait_all(ref, send_sem.at[kind], recv_sem.at[kind])

    first_row = gy * ROWS
    first_col = gx * COLS
    total_rows, total_cols = ny * ROWS, nx * COLS

    def framed(row, rows, middle, west, east):
        n = lane_index(rows, 128)
        moved = pltpu.roll(middle, PLANE_MARGIN, 1)
        low = jnp.where(n < PLANE_MARGIN, west, moved)
        high = jnp.where(n < PLANE_MARGIN, moved, jnp.where(n < 2 * PLANE_MARGIN, pltpu.roll(east, 54, 1), 0.0))
        value = jnp.concatenate([low, high], axis=1)
        y = first_row - PLANE_MARGIN - 2 + row + row_index(rows)
        x = first_col - PLANE_MARGIN + lane_index(rows)
        inside = (y >= 0) & (y < total_rows) & (x >= 0) & (x < total_cols)
        plane[row : row + rows, :] = pltpu.roll(jnp.where(inside, value, 0.0), LANES - TAPS + 1 - 4, 1)

    def wide(value):
        return value.astype(F32)

    framed(0, 16, wide(got_rims[1, 0]), wide(got_rims[0, 0]), wide(got_rims[2, 0]))
    framed(16, 40, wide(got_whole[0, 0]), wide(got_edges[0, 0]), wide(got_edges[1, 0]))
    framed(56, 40, own_plane, wide(got_edges[0, 1]), wide(got_edges[1, 1]))
    framed(96, 40, wide(got_whole[1, 0]), wide(got_edges[0, 2]), wide(got_edges[1, 2]))
    framed(136, 16, wide(got_rims[1, 1]), wide(got_rims[0, 1]), wide(got_rims[2, 1]))
    plane[152:160, :] = jnp.zeros((8, LANES), F32)

    def framed_target(row, middle, west, east):
        n = lane_index(ROWS, 128)
        moved = pltpu.roll(middle, FIELD_MARGIN, 1)
        wanted[0, row : row + ROWS, :] = jnp.where(n < FIELD_MARGIN, pltpu.roll(west, 74, 1), moved)
        wanted[1, row : row + ROWS, :] = jnp.where(n < FIELD_MARGIN, moved, pltpu.roll(east, 101, 1))

    framed_target(0, wide(got_whole[0, 1]), wide(got_edges[0, 0]), wide(got_edges[1, 0]))
    framed_target(40, own_target, wide(got_edges[0, 1]), wide(got_edges[1, 1]))
    framed_target(80, wide(got_whole[1, 1]), wide(got_edges[0, 2]), wide(got_edges[1, 2]))

    n8 = row_index(8)

    def spread(chunk):
        for v in range(chunk * 8, chunk * 8 + 8, 4):
            pieces = []
            for u in (v, v + 2):
                even = jnp.broadcast_to(plane[u + 2 : u + 3, :], (40, LANES))
                odd = jnp.broadcast_to(plane[u + 3 : u + 4, :], (40, LANES))
                even = pltpu.roll(even, 4, 1, stride=1, stride_axis=0)
                odd = pltpu.roll(odd, 0, 1, stride=1, stride_axis=0)
                pieces += [even[0:32], jnp.where(n8 < 4, even[32:40], odd[0:8]), odd[8:40]]
            patches[v * PITCH : (v + 4) * PITCH, :] = jnp.concatenate(pieces, axis=0).astype(BF16)

    for chunk in range(6):
        spread(chunk)

    def inside_field(start, rows):
        y = first_row - FIELD_MARGIN + start + row_index(rows)
        x = first_col - FIELD_MARGIN + lane_index(rows)
        return (y >= 0) & (y < total_rows) & (x >= 0) & (x < total_cols)

    def band(i):
        first = i * BAND * PITCH
        value = jnp.dot(taps[...], patches[first : first + DEPTH, :], preferred_element_type=F32)
        value = value.reshape(CHANNELS, BAND, LANES)
        start = i * BAND
        if FIRST_BAND <= i <= LAST_BAND:
            field[:, start : start + BAND, :] = value
        intensity = jnp.sum(value * value, axis=0) / KERNELS
        rows_to(dim, start + 6, jnp.where(inside_field(start, BAND), intensity, 0.0))

    for i in range(BANDS):
        if i + 6 < 19:
            spread(i + 6)
        band(i)
        if i == 9:
            learn(2)
            tell(3)

    dense = smooth(dim, 8, 112)
    rows_to(lit, 8, jnp.where(inside_field(2, 112), jax.nn.sigmoid(SHARPNESS * (dense - THRESHOLD)), 0.0))

    loading = jnp.zeros((96, LANES), F32)
    for j in range(LOAD_TAPS):
        part = rows_from(lit, 16 + offsets_ref[0, j], 96)
        loading = loading + weights_ref[j] * pltpu.roll(part, lax.rem(LANES - offsets_ref[1, j], LANES), 1)
    printed = rows_from(lit, 16, 96) - LOADING_GAIN / LOAD_TAPS * loading
    y = first_row - FIELD_MARGIN + 10 + row_index(96)
    x = first_col - FIELD_MARGIN + lane_index(96)
    weight = (1.0 + 2.0 * y.astype(F32) / total_rows) * (1.0 + 2.0 * x.astype(F32) / total_cols)
    diff = printed - rows_from(wanted, 13, 96)
    own = (y >= first_row) & (y < first_row + ROWS) & (x >= first_col) & (x < first_col + COLS)
    loss = jnp.sum(jnp.where(own, weight * diff * diff, 0.0), axis=0, keepdims=True)
    rows_to(rest, 16, jnp.where(inside_field(10, 96), 2.0 * weight * diff, 0.0))

    back = jnp.zeros((80, LANES), F32)
    for j in range(LOAD_TAPS):
        part = rows_from(rest, 24 - offsets_ref[0, j], 80)
        back = back + weights_ref[j] * pltpu.roll(part, lax.rem(LANES + offsets_ref[1, j], LANES), 1)
    slope = rows_from(rest, 24, 80) - LOADING_GAIN / LOAD_TAPS * back
    nearby = rows_from(lit, 24, 80)
    rows_to(dim, 24, slope * SHARPNESS * nearby * (1.0 - nearby))
    rows_to(pull, 24, jnp.where(inside_field(18, 80), (2.0 / KERNELS) * smooth(dim, 24, 80), 0.0))

    def weigh(i):
        start = (i + FIRST_BAND) * BAND
        value = field[:, start : start + BAND, :] * rows_from(pull, start + 6, BAND)[None]
        rows = CHANNELS * BAND
        products[i * rows : (i + 1) * rows, :] = value.reshape(rows, LANES).astype(BF16)

    def mix(g):
        rows = CHANNELS * BAND
        value = jnp.dot(mixer[...], products[g * rows : (g + 6) * rows, :], preferred_element_type=F32)
        for i in range(2):
            mixed[i, g * 8 * PITCH : (g + 1) * 8 * PITCH, :] = value[:, i * 128 : (i + 1) * 128]

    def gather_taps(g):
        total = jnp.zeros((8, LANES), F32)
        for t in range(TAPS):
            rows = pl.ds(g * 8 * PITCH + t, 8, stride=PITCH)
            part = jnp.concatenate([mixed[i, rows, :] for i in range(2)], axis=1)
            total = total + pltpu.roll(part, 236 - t, 1)
        return total[:, 0:128]

    for i in range(5):
        weigh(i)
    parts = []
    for g in range(ROWS // 8):
        weigh(g + 5)
        mix(g)
        if g:
            parts.append(gather_taps(g - 1))
    parts.append(gather_taps(ROWS // 8 - 1))
    gradient = jnp.concatenate(parts, axis=0)

    inner = max(d for d in (1, 2, 4) if nx % d == 0)
    outer = nx // inner

    def ring(d, n):
        return min(d, n - d)

    def gather(sums, number):
        if number == 0:
            hops = [(ring(d, ny), d, 0) for d in range(1, ny)]
        else:
            hops = [(ring(a, outer) + ring(b, inner), a, b) for a in range(outer) for b in range(inner) if a or b]
        me = gx if number else gy
        for _, a, b in sorted(hops, reverse=True):
            if number == 0:
                device = at(a, 0)
            else:
                y, x = lax.rem(gx // inner + a, outer), lax.rem(lax.rem(gx, inner) + b, inner)
                device = (gy, y * inner + x)
            pltpu.make_async_remote_copy(
                src_ref=sums.at[me],
                dst_ref=sums.at[me],
                send_sem=sum_send.at[number],
                recv_sem=sum_recv.at[number],
                device_id=device,
                device_id_type=MESH,
            ).start()
        wait_all(sums.at[pl.ds(0, len(hops))], sum_send.at[number], sum_recv.at[number])

    gradient_ref[...] = gradient
    square = jnp.sum(gradient * gradient, axis=0, keepdims=True)
    sums_y[gy, 0:1, :] = loss[:, 0:128] + loss[:, 128:256]
    sums_y[gy, 1:2, :] = square
    gather(sums_y, 0)
    learn(3)
    sums_x[gx] = jnp.sum(sums_y[...], axis=0)
    gather(sums_x, 1)
    sums_ref[...] = jnp.sum(sums_x[...], axis=0)


def finish(pixels, mask_ref, gradient_ref, sums_ref, update_ref, loss_ref):
    totals = jnp.sum(sums_ref[...], axis=1, keepdims=True)
    loss_ref[...] = totals[0:1, :]
    scale = jnp.sqrt(totals[1:2, :] / pixels + 1e-06)
    update_ref[...] = mask_ref[...] - gradient_ref[...] / scale


def solution(mesh):
    ny, nx = mesh.shape["gy"], mesh.shape["gx"]
    vmem = pl.BlockSpec(memory_space=pltpu.VMEM)
    rows = CHANNELS * BAND

    def step(mask, target, kernels, offsets, load_weights):
        held, gradient, sums = pl.pallas_call(
            functools.partial(kernel, (ny, nx)),
            out_shape=(
                pltpu.VMEM((ROWS, COLS), F32),
                pltpu.VMEM((ROWS, COLS), F32),
                pltpu.VMEM((2, 128), F32),
            ),
            in_specs=[pl.BlockSpec(memory_space=pl.ANY)] * 5,
            out_specs=(vmem, vmem, vmem),
            scratch_shapes=[
                pltpu.SMEM((2, LOAD_TAPS), jnp.int32),
                pltpu.SMEM((LOAD_TAPS,), F32),
                pltpu.VMEM((ROWS, COLS), jnp.int32),
                pltpu.VMEM((TAPS, CHANNELS, TAPS), BF16),
                pltpu.SemaphoreType.DMA((5,)),
                pltpu.VMEM((2, ROWS, COLS), BF16),
                pltpu.VMEM((2, ROWS, COLS), BF16),
                pltpu.VMEM((3, 2, 16, COLS), BF16),
                pltpu.VMEM((2, 2, ROWS, COLS), BF16),
                pltpu.VMEM((2, 3, ROWS, COLS), BF16),
                pltpu.VMEM((3, 2, 16, COLS), BF16),
                pltpu.VMEM((ny, 2, 128), F32),
                pltpu.VMEM((nx, 2, 128), F32),
                pltpu.VMEM((DEPTH // 128, rows, 128), F32),
                pltpu.VMEM((rows, DEPTH), BF16),
                pltpu.VMEM((6 * rows, 384), F32),
                pltpu.VMEM((8 * PITCH, 6 * rows), BF16),
                pltpu.VMEM((160, LANES), F32),
                pltpu.VMEM((2, 120, 128), F32),
                pltpu.VMEM((152 * PITCH + 96, LANES), BF16),
                pltpu.VMEM((CHANNELS, BANDS * BAND, LANES), F32),
                pltpu.VMEM((2, 128, 128), F32),
                pltpu.VMEM((2, 128, 128), F32),
                pltpu.VMEM((2, 128, 128), F32),
                pltpu.VMEM((2, 128, 128), F32),
                pltpu.VMEM((10 * rows, LANES), BF16),
                pltpu.VMEM((2, ROWS * PITCH, 128), F32),
                pltpu.SemaphoreType.DMA((3,)),
                pltpu.SemaphoreType.DMA((3,)),
                pltpu.SemaphoreType.DMA((2,)),
                pltpu.SemaphoreType.DMA((2,)),
                pltpu.SemaphoreType.REGULAR((2, 4)),
            ],
            compiler_params=pltpu.CompilerParams(collective_id=0, has_side_effects=True),
        )(offsets.T, load_weights, mask, target, kernels.transpose(1, 0, 2))
        update, loss = pl.pallas_call(
            functools.partial(finish, ny * ROWS * nx * COLS),
            out_shape=(
                jax.ShapeDtypeStruct((ROWS, COLS), F32),
                jax.ShapeDtypeStruct((1, 1), F32),
            ),
            in_specs=[vmem] * 3,
            out_specs=(vmem, vmem),
        )(*(pltpu.with_memory_space_constraint(a, pltpu.VMEM) for a in (held, gradient, sums)))
        return update, loss[0, 0]

    placed = (P("gy", "gx"), P("gy", "gx"), P(), P(), P())
    return jax.shard_map(step, mesh=mesh, in_specs=placed, out_specs=(P("gy", "gx"), P()), check_vma=False)
```

```python
import functools

import jax
import jax.numpy as jnp
from jax import lax
from jax.experimental import pallas as pl
from jax.experimental.pallas import tpu as pltpu
from jax.sharding import PartitionSpec as P

MESH = pl.DeviceIdType.MESH
F32 = jnp.float32
BF16 = jnp.bfloat16

KERNELS = 12
CHANNELS = 24
TAPS = 35
REACH = 8
LOAD_TAPS = 8
SMOOTH_TAPS = (0.0625, 0.25, 0.375, 0.25, 0.0625)
SHARPNESS = 4.0
THRESHOLD = 0.65
LOADING_GAIN = 0.5

ROWS, COLS = 40, 128
LANES = 256
FIELD_MARGIN = 37
PLANE_MARGIN = 54
PITCH = 36
BAND = 8
DEPTH = 1536
BANDS = 15
FIRST_BAND, LAST_BAND = 2, 11


def lane_index(rows, lanes=LANES):
    return lax.broadcasted_iota(jnp.int32, (rows, lanes), 1)


def row_index(rows, lanes=LANES):
    return lax.broadcasted_iota(jnp.int32, (rows, lanes), 0)


def rows_from(halves, start, rows):
    return jnp.concatenate([halves[i, pl.ds(start, rows), :] for i in range(2)], axis=1)


def rows_to(halves, start, value):
    for i in range(2):
        halves[i, start : start + value.shape[0], :] = value[:, i * 128 : (i + 1) * 128]


def smooth(halves, start, rows):
    down = sum(SMOOTH_TAPS[a] * rows_from(halves, start + a - 2, rows) for a in range(5))
    total = SMOOTH_TAPS[2] * down
    for b in (0, 1, 3, 4):
        total = total + SMOOTH_TAPS[b] * pltpu.roll(down, (2 - b) % LANES, 1)
    return total


def build_taps(kernels_ref, taps32, taps):
    flip = (
        lax.broadcasted_iota(jnp.int32, (TAPS, 128), 0) + lax.broadcasted_iota(jnp.int32, (TAPS, 128), 1) == TAPS - 1
    ).astype(BF16)
    lane = lane_index(CHANNELS, 128)
    tiles = [jnp.zeros((CHANNELS, 128), F32) for _ in range(DEPTH // 128)]
    for a in range(TAPS):
        tile, shift = divmod(a * PITCH, 128)
        row = jnp.dot(kernels_ref[a], flip, preferred_element_type=F32)
        moved = pltpu.roll(row, shift, 1) if shift else row
        tiles[tile] = tiles[tile] + jnp.where(lane >= shift, moved, 0.0)
        if shift + TAPS > 128:
            tiles[tile + 1] = tiles[tile + 1] + jnp.where(lane < shift, moved, 0.0)
    base = jnp.concatenate(tiles, axis=1)
    for y in range(BAND):
        moved = pltpu.roll(base, y * PITCH, 1) if y else base
        for i in range(DEPTH // 128):
            taps32[i, pl.ds(y, CHANNELS, stride=BAND), :] = moved[:, i * 128 : (i + 1) * 128]
    for i in range(DEPTH // 128):
        taps[:, i * 128 : (i + 1) * 128] = taps32[i].astype(BF16)


def build_mixer(taps32, mixer32, mixer):
    joined = jnp.concatenate([taps32[i] for i in range(DEPTH // 128)], axis=1)
    rows = CHANNELS * BAND
    for n in range(6):
        first = (PLANE_MARGIN - 8 * (n + 2)) * PITCH
        low, high = max(first, 0), min(first + 8 * PITCH, DEPTH)
        window = joined[:, low:high]
        if first < 0:
            window = jnp.concatenate([jnp.zeros((rows, -first), F32), window], axis=1)
        if high < first + 8 * PITCH:
            window = jnp.concatenate([window, jnp.zeros((rows, first + 8 * PITCH - high), F32)], axis=1)
        mixer32[n * rows : (n + 1) * rows, 0 : 8 * PITCH] = window
    mixer[...] = mixer32[...].T[0 : 8 * PITCH, :].astype(BF16)


def kernel(
    sizes,
    offsets_hbm,
    weights_hbm,
    mask_hbm,
    target_hbm,
    kernels_hbm,
    mask_ref,
    gradient_ref,
    sums_ref,
    offsets_ref,
    weights_ref,
    target_ref,
    kernels_ref,
    input_sem,
    whole,
    edges,
    rims,
    got_whole,
    got_edges,
    got_rims,
    sums_y,
    sums_x,
    taps32,
    taps,
    mixer32,
    mixer,
    plane,
    wanted,
    patches,
    field,
    dim,
    lit,
    rest,
    pull,
    products,
    mixed,
    send_sem,
    recv_sem,
    sum_send,
    sum_recv,
    known,
):
    ny, nx = sizes
    gy, gx = lax.axis_index("gy"), lax.axis_index("gx")

    def at(dy, dx):
        return (lax.rem(gy + (dy % ny), ny), lax.rem(gx + (dx % nx), nx))

    inputs = [
        pltpu.make_async_copy(source, target, input_sem.at[i])
        for i, (source, target) in enumerate(
            (
                (mask_hbm, mask_ref),
                (target_hbm, target_ref),
                (kernels_hbm, kernels_ref),
                (offsets_hbm, offsets_ref),
                (weights_hbm, weights_ref),
            )
        )
    ]
    for copy in inputs:
        copy.start()
    peers = sorted({(dy % ny, dx % nx) for dy in range(-2, 3) for dx in range(-1, 2)} - {(0, 0)})
    barrier = pltpu.get_barrier_semaphore()
    for dy, dx in peers:
        pl.semaphore_signal(barrier, inc=1, device_id=at(dy, dx), device_id_type=MESH)

    rounds_y = [r for r in (4, 8) if 2 * r < ny]
    rounds_x = [r for r in (2, 4, 8) if 2 * r < nx]

    def tell(number):
        for along_x, rounds in ((0, rounds_y), (1, rounds_x)):
            if number < len(rounds):
                for r in (rounds[number], -rounds[number]):
                    pl.semaphore_signal(
                        known.at[along_x, number],
                        inc=1,
                        device_id=at(0, r) if along_x else at(r, 0),
                        device_id_type=MESH,
                    )

    def learn(number):
        for along_x, rounds in ((0, rounds_y), (1, rounds_x)):
            if number < len(rounds):
                pl.semaphore_wait(known.at[along_x, number], 2)

    inputs[0].wait()
    inputs[1].wait()

    own_plane = mask_ref[...].astype(BF16).astype(F32)
    own_target = target_ref[...].astype(F32)
    lane = lane_index(ROWS, 128)
    whole[0] = own_plane.astype(BF16)
    whole[1] = own_target.astype(BF16)
    left = jnp.where(lane < 64, own_plane, pltpu.roll(own_target, 64, 1))
    right = jnp.where(lane < 64, pltpu.roll(own_plane, 54, 1), pltpu.roll(own_target, 91, 1))
    edges[0] = left.astype(BF16)
    edges[1] = right.astype(BF16)
    for i, value in enumerate((right, own_plane, left)):
        rims[i, 0] = value[24:40, :].astype(BF16)
        rims[i, 1] = value[0:16, :].astype(BF16)

    pl.semaphore_wait(barrier, len(peers))

    def send(kind, source, target, dy, dx):
        pltpu.make_async_remote_copy(
            src_ref=source,
            dst_ref=target,
            send_sem=send_sem.at[kind],
            recv_sem=recv_sem.at[kind],
            device_id=at(dy, dx),
            device_id_type=MESH,
        ).start()

    def send_rim(dy, dx):
        end = 0 if dy == 2 else 1
        send(1, rims.at[1 - dx, end], got_rims.at[1 - dx, end], dy, dx)

    def wait_all(ref, sent, received):
        for sem in (sent, received):
            pltpu.make_async_copy(ref, ref, sem).wait()

    for dx in (1, -1):
        for dy in (2, -2):
            send_rim(dy, dx)
    for dy in (-1, 1, 0):
        for dx in (1, -1):
            side = 0 if dx == 1 else 1
            send(0, edges.at[1 - side], got_edges.at[side, 1 - dy], dy, dx)
    for dy in (1, -1):
        send(2, whole, got_whole.at[0 if dy == 1 else 1], dy, 0)
    for dy in (2, -2):
        send_rim(dy, 0)
    inputs[2].wait()
    build_taps(kernels_ref, taps32, taps)
    build_mixer(taps32, mixer32, mixer)
    inputs[3].wait()
    inputs[4].wait()
    rows_to(pull, 16, jnp.zeros((8, LANES), F32))
    patches[152 * PITCH :, :] = jnp.zeros((96, LANES), BF16)
    for kind, ref in enumerate((got_edges, got_rims, got_whole)):
        wait_all(ref, send_sem.at[kind], recv_sem.at[kind])
    tell(0)

    first_row = gy * ROWS
    first_col = gx * COLS
    total_rows, total_cols = ny * ROWS, nx * COLS

    def framed(row, rows, middle, west, east):
        n = lane_index(rows, 128)
        moved = pltpu.roll(middle, PLANE_MARGIN, 1)
        low = jnp.where(n < PLANE_MARGIN, west, moved)
        high = jnp.where(n < PLANE_MARGIN, moved, jnp.where(n < 2 * PLANE_MARGIN, pltpu.roll(east, 54, 1), 0.0))
        value = jnp.concatenate([low, high], axis=1)
        y = first_row - PLANE_MARGIN - 2 + row + row_index(rows)
        x = first_col - PLANE_MARGIN + lane_index(rows)
        inside = (y >= 0) & (y < total_rows) & (x >= 0) & (x < total_cols)
        plane[row : row + rows, :] = pltpu.roll(jnp.where(inside, value, 0.0), LANES - TAPS + 1 - 4, 1)

    def wide(value):
        return value.astype(F32)

    framed(0, 16, wide(got_rims[1, 0]), wide(got_rims[0, 0]), wide(got_rims[2, 0]))
    framed(16, 40, wide(got_whole[0, 0]), wide(got_edges[0, 0]), wide(got_edges[1, 0]))
    framed(56, 40, own_plane, wide(got_edges[0, 1]), wide(got_edges[1, 1]))
    framed(96, 40, wide(got_whole[1, 0]), wide(got_edges[0, 2]), wide(got_edges[1, 2]))
    framed(136, 16, wide(got_rims[1, 1]), wide(got_rims[0, 1]), wide(got_rims[2, 1]))
    plane[152:160, :] = jnp.zeros((8, LANES), F32)

    def framed_target(row, middle, west, east):
        n = lane_index(ROWS, 128)
        moved = pltpu.roll(middle, FIELD_MARGIN, 1)
        wanted[0, row : row + ROWS, :] = jnp.where(n < FIELD_MARGIN, pltpu.roll(west, 74, 1), moved)
        wanted[1, row : row + ROWS, :] = jnp.where(n < FIELD_MARGIN, moved, pltpu.roll(east, 101, 1))

    framed_target(0, wide(got_whole[0, 1]), wide(got_edges[0, 0]), wide(got_edges[1, 0]))
    framed_target(40, own_target, wide(got_edges[0, 1]), wide(got_edges[1, 1]))
    framed_target(80, wide(got_whole[1, 1]), wide(got_edges[0, 2]), wide(got_edges[1, 2]))

    n8 = row_index(8)

    def spread(chunk):
        for v in range(chunk * 8, chunk * 8 + 8, 4):
            pieces = []
            for u in (v, v + 2):
                even = jnp.broadcast_to(plane[u + 2 : u + 3, :], (40, LANES))
                odd = jnp.broadcast_to(plane[u + 3 : u + 4, :], (40, LANES))
                even = pltpu.roll(even, 4, 1, stride=1, stride_axis=0)
                odd = pltpu.roll(odd, 0, 1, stride=1, stride_axis=0)
                pieces += [even[0:32], jnp.where(n8 < 4, even[32:40], odd[0:8]), odd[8:40]]
            patches[v * PITCH : (v + 4) * PITCH, :] = jnp.concatenate(pieces, axis=0).astype(BF16)

    for chunk in range(6):
        spread(chunk)

    def inside_field(start, rows):
        y = first_row - FIELD_MARGIN + start + row_index(rows)
        x = first_col - FIELD_MARGIN + lane_index(rows)
        return (y >= 0) & (y < total_rows) & (x >= 0) & (x < total_cols)

    def band(i):
        first = i * BAND * PITCH
        value = jnp.dot(taps[...], patches[first : first + DEPTH, :], preferred_element_type=F32)
        value = value.reshape(CHANNELS, BAND, LANES)
        start = i * BAND
        if FIRST_BAND <= i <= LAST_BAND:
            field[:, start : start + BAND, :] = value
        intensity = jnp.sum(value * value, axis=0) / KERNELS
        rows_to(dim, start + 6, jnp.where(inside_field(start, BAND), intensity, 0.0))

    for i in range(BANDS):
        if i + 6 < 19:
            spread(i + 6)
        band(i)
    learn(0)
    tell(1)

    dense = smooth(dim, 8, 112)
    rows_to(lit, 8, jnp.where(inside_field(2, 112), jax.nn.sigmoid(SHARPNESS * (dense - THRESHOLD)), 0.0))

    loading = jnp.zeros((96, LANES), F32)
    for j in range(LOAD_TAPS):
        part = rows_from(lit, 16 + offsets_ref[0, j], 96)
        loading = loading + weights_ref[j] * pltpu.roll(part, lax.rem(LANES - offsets_ref[1, j], LANES), 1)
    printed = rows_from(lit, 16, 96) - LOADING_GAIN / LOAD_TAPS * loading
    y = first_row - FIELD_MARGIN + 10 + row_index(96)
    x = first_col - FIELD_MARGIN + lane_index(96)
    weight = (1.0 + 2.0 * y.astype(F32) / total_rows) * (1.0 + 2.0 * x.astype(F32) / total_cols)
    diff = printed - rows_from(wanted, 13, 96)
    own = (y >= first_row) & (y < first_row + ROWS) & (x >= first_col) & (x < first_col + COLS)
    loss = jnp.sum(jnp.where(own, weight * diff * diff, 0.0), axis=0, keepdims=True)
    rows_to(rest, 16, jnp.where(inside_field(10, 96), 2.0 * weight * diff, 0.0))

    back = jnp.zeros((80, LANES), F32)
    for j in range(LOAD_TAPS):
        part = rows_from(rest, 24 - offsets_ref[0, j], 80)
        back = back + weights_ref[j] * pltpu.roll(part, lax.rem(LANES + offsets_ref[1, j], LANES), 1)
    slope = rows_from(rest, 24, 80) - LOADING_GAIN / LOAD_TAPS * back
    nearby = rows_from(lit, 24, 80)
    rows_to(dim, 24, slope * SHARPNESS * nearby * (1.0 - nearby))
    rows_to(pull, 24, jnp.where(inside_field(18, 80), (2.0 / KERNELS) * smooth(dim, 24, 80), 0.0))

    def weigh(i):
        start = (i + FIRST_BAND) * BAND
        value = field[:, start : start + BAND, :] * rows_from(pull, start + 6, BAND)[None]
        rows = CHANNELS * BAND
        products[i * rows : (i + 1) * rows, :] = value.reshape(rows, LANES).astype(BF16)

    def mix(g):
        rows = CHANNELS * BAND
        value = jnp.dot(mixer[...], products[g * rows : (g + 6) * rows, :], preferred_element_type=F32)
        for i in range(2):
            mixed[i, g * 8 * PITCH : (g + 1) * 8 * PITCH, :] = value[:, i * 128 : (i + 1) * 128]

    def gather_taps(g):
        total = jnp.zeros((8, LANES), F32)
        for t in range(TAPS):
            rows = pl.ds(g * 8 * PITCH + t, 8, stride=PITCH)
            part = jnp.concatenate([mixed[i, rows, :] for i in range(2)], axis=1)
            total = total + pltpu.roll(part, 236 - t, 1)
        return total[:, 0:128]

    for i in range(5):
        weigh(i)
    parts = []
    for g in range(ROWS // 8):
        weigh(g + 5)
        mix(g)
        if g:
            parts.append(gather_taps(g - 1))
    parts.append(gather_taps(ROWS // 8 - 1))
    gradient = jnp.concatenate(parts, axis=0)

    inner = max(d for d in (1, 2, 4) if nx % d == 0)
    outer = nx // inner

    def ring(d, n):
        return min(d, n - d)

    def gather(sums, number):
        if number == 0:
            hops = [(ring(d, ny), d, 0) for d in range(1, ny)]
        else:
            hops = [(ring(a, outer) + ring(b, inner), a, b) for a in range(outer) for b in range(inner) if a or b]
        me = gx if number else gy
        for _, a, b in sorted(hops, reverse=True):
            if number == 0:
                device = at(a, 0)
            else:
                y, x = lax.rem(gx // inner + a, outer), lax.rem(lax.rem(gx, inner) + b, inner)
                device = (gy, y * inner + x)
            pltpu.make_async_remote_copy(
                src_ref=sums.at[me],
                dst_ref=sums.at[me],
                send_sem=sum_send.at[number],
                recv_sem=sum_recv.at[number],
                device_id=device,
                device_id_type=MESH,
            ).start()
        wait_all(sums.at[pl.ds(0, len(hops))], sum_send.at[number], sum_recv.at[number])

    gradient_ref[...] = gradient
    square = jnp.sum(gradient * gradient, axis=0, keepdims=True)
    sums_y[gy, 0:1, :] = loss[:, 0:128] + loss[:, 128:256]
    sums_y[gy, 1:2, :] = square
    learn(1)
    tell(2)
    gather(sums_y, 0)
    learn(2)
    sums_x[gx] = jnp.sum(sums_y[...], axis=0)
    gather(sums_x, 1)
    sums_ref[...] = jnp.sum(sums_x[...], axis=0)


def finish(pixels, mask_ref, gradient_ref, sums_ref, update_ref, loss_ref):
    totals = jnp.sum(sums_ref[...], axis=1, keepdims=True)
    loss_ref[...] = totals[0:1, :]
    scale = jnp.sqrt(totals[1:2, :] / pixels + 1e-06)
    update_ref[...] = mask_ref[...] - gradient_ref[...] / scale


def solution(mesh):
    ny, nx = mesh.shape["gy"], mesh.shape["gx"]
    vmem = pl.BlockSpec(memory_space=pltpu.VMEM)
    rows = CHANNELS * BAND

    def step(mask, target, kernels, offsets, load_weights):
        held, gradient, sums = pl.pallas_call(
            functools.partial(kernel, (ny, nx)),
            out_shape=(
                pltpu.VMEM((ROWS, COLS), F32),
                pltpu.VMEM((ROWS, COLS), F32),
                pltpu.VMEM((2, 128), F32),
            ),
            in_specs=[pl.BlockSpec(memory_space=pl.ANY)] * 5,
            out_specs=(vmem, vmem, vmem),
            scratch_shapes=[
                pltpu.SMEM((2, LOAD_TAPS), jnp.int32),
                pltpu.SMEM((LOAD_TAPS,), F32),
                pltpu.VMEM((ROWS, COLS), jnp.int32),
                pltpu.VMEM((TAPS, CHANNELS, TAPS), BF16),
                pltpu.SemaphoreType.DMA((5,)),
                pltpu.VMEM((2, ROWS, COLS), BF16),
                pltpu.VMEM((2, ROWS, COLS), BF16),
                pltpu.VMEM((3, 2, 16, COLS), BF16),
                pltpu.VMEM((2, 2, ROWS, COLS), BF16),
                pltpu.VMEM((2, 3, ROWS, COLS), BF16),
                pltpu.VMEM((3, 2, 16, COLS), BF16),
                pltpu.VMEM((ny, 2, 128), F32),
                pltpu.VMEM((nx, 2, 128), F32),
                pltpu.VMEM((DEPTH // 128, rows, 128), F32),
                pltpu.VMEM((rows, DEPTH), BF16),
                pltpu.VMEM((6 * rows, 384), F32),
                pltpu.VMEM((8 * PITCH, 6 * rows), BF16),
                pltpu.VMEM((160, LANES), F32),
                pltpu.VMEM((2, 120, 128), F32),
                pltpu.VMEM((152 * PITCH + 96, LANES), BF16),
                pltpu.VMEM((CHANNELS, BANDS * BAND, LANES), F32),
                pltpu.VMEM((2, 128, 128), F32),
                pltpu.VMEM((2, 128, 128), F32),
                pltpu.VMEM((2, 128, 128), F32),
                pltpu.VMEM((2, 128, 128), F32),
                pltpu.VMEM((10 * rows, LANES), BF16),
                pltpu.VMEM((2, ROWS * PITCH, 128), F32),
                pltpu.SemaphoreType.DMA((3,)),
                pltpu.SemaphoreType.DMA((3,)),
                pltpu.SemaphoreType.DMA((2,)),
                pltpu.SemaphoreType.DMA((2,)),
                pltpu.SemaphoreType.REGULAR((2, 3)),
            ],
            compiler_params=pltpu.CompilerParams(collective_id=0, has_side_effects=True),
        )(offsets.T, load_weights, mask, target, kernels.transpose(1, 0, 2))
        update, loss = pl.pallas_call(
            functools.partial(finish, ny * ROWS * nx * COLS),
            out_shape=(
                jax.ShapeDtypeStruct((ROWS, COLS), F32),
                jax.ShapeDtypeStruct((1, 1), F32),
            ),
            in_specs=[vmem] * 3,
            out_specs=(vmem, vmem),
        )(*(pltpu.with_memory_space_constraint(a, pltpu.VMEM) for a in (held, gradient, sums)))
        return update, loss[0, 0]

    placed = (P("gy", "gx"), P("gy", "gx"), P(), P(), P())
    return jax.shard_map(step, mesh=mesh, in_specs=placed, out_specs=(P("gy", "gx"), P()), check_vma=False)
```
